512 devices in a mesh: req: 128 (over z, y, core), tp: 4 (over x).
Axes of the slice: x: 4, y: 8, z: 8, core: 2. Of those that a mesh axis runs over, the one named last changes fastest.
Arguments:
- tokens: bfloat16 [49152, 3200], P('req'), may hold values from -6 to 6
- norm_gain: float32 [3200], replicated, may hold values from 0.5 to 2
- w_qkv: bfloat16 [3200, 6144], P('req', 'tp'), may hold values from -1 to 1
- q_gain: float32 [2048], P('tp'), may hold values from 0.5 to 2.5
- k_gain: float32 [2048], P('tp'), may hold values from 0.5 to 2.5
- w_out: bfloat16 [2048, 3200], P('tp', 'req'), may hold values from -0.125 to 0.125
- grids: int32 [384, 2], P('req'), may hold values from 2 to 16, as said below
- owners: int32 [12288], P('req'), may hold values from 0 to 127, as said below
- proj_gain: float32 [4, 3200], P(None, 'tp'), may hold values from 0.5 to 2
- proj_bias: float32 [4, 3200], P(None, 'tp'), may hold values from -3 to 3
Outputs:
- received: bfloat16 [32768, 4, 3200], P('req', None, 'tp')
The draws below stay inside these ranges and needn't reach their ends.
Inputs may be any that keep to these rules, and one draw needn't show every extreme that they name: `grids`: each image spans at least 2 half grid rows. The images of one device together take at most 96 merged slots, and on one device in every draw exactly 96. `owners`: no device's merged slots, live or padding, name one owner more than 2 times; in every draw one owner is named exactly 2 times by every device.
All inputs are finite; a program needn't handle non-finite values.
Results may differ from the reference program's by a relative error of at most 0.009.
Values may be sent and summed in bfloat16 or wider, within the bound.
A program may use at most 128 MiB of HBM per device.

```python
import math
import jax
import jax.numpy as jnp
from jax import lax

D = 3200
HEADS = 16
HEAD_DIM = 128
IMG_DEV = 3
TOK_DEV = 384
MRG_DEV = 96
CAP = 2
TOKENS = 49152
N_REQ = 128
N_TP = 4


def draw_tokens(key, part):
    values = jnp.clip(jax.random.normal(jax.random.fold_in(key, 1), (TOKENS, D), jnp.float32), -6.0, 6.0)
    return values.astype(jnp.bfloat16)


def draw_w_qkv(key, part):
    scale = 1.0 / math.sqrt(D)
    values = jnp.clip(jax.random.normal(jax.random.fold_in(key, 3), (D, HEADS, 3, HEAD_DIM), jnp.float32), -6.0, 6.0) * scale
    return jnp.clip(values, -1.0, 1.0).reshape(D, 3 * HEADS * HEAD_DIM).astype(jnp.bfloat16)


def draw_grids(key, part):
    device_count = TOKENS // TOK_DEV
    third = MRG_DEV // 3
    key_rows, key_cols, key_full = jax.random.split(key, 3)
    half_rows = 2 * jax.random.randint(key_rows, (device_count, 3), 1, 3)
    widest = third // half_rows
    half_cols = jnp.maximum(widest - jax.random.randint(key_cols, (device_count, 3), 0, 2), 1)
    full_device = jax.random.randint(key_full, (), 0, device_count)
    chosen = jnp.arange(device_count) == full_device
    full_rows = jnp.array([2, 2, 4], jnp.int32)
    full_cols = jnp.array([MRG_DEV // 6, MRG_DEV // 6, MRG_DEV // 12], jnp.int32)
    half_rows = jnp.where(chosen[:, None], full_rows[None, :], half_rows)
    half_cols = jnp.where(chosen[:, None], full_cols[None, :], half_cols)
    return jnp.stack([half_rows, half_cols], axis=-1).reshape(device_count * 3, 2).astype(jnp.int32)


def draw_owners(key, part):
    device_count = TOKENS // TOK_DEV
    key_full, key_rest = jax.random.split(key)
    full_owner = jax.random.randint(key_full, (), 0, device_count)
    source_keys = jax.random.split(key_rest, device_count)

    def one_source(source_key):
        picked = jax.random.permutation(source_key, (device_count - 1) * CAP)[:MRG_DEV - CAP]
        shifted = picked + CAP * (picked // CAP >= full_owner).astype(picked.dtype)
        head_part = jnp.full((CAP,), full_owner, dtype=picked.dtype)
        return jnp.concatenate([head_part, shifted // CAP])
    return jax.vmap(one_source)(source_keys).reshape(-1).astype(jnp.int32)


def shard_levels(rng, extent, pieces, smallest, top_value):
    def one(axis_at, blocks):
        heights = jax.random.uniform(jax.random.fold_in(jax.random.fold_in(rng, 6), axis_at), (blocks,), jnp.float32, smallest / len(pieces), top_value / len(pieces))
        return jnp.repeat(jnp.exp(heights), extent[axis_at] // blocks).reshape((-1,) + (1,) * (len(extent) - axis_at - 1))

    gain = one(*pieces[0])
    for cut in pieces[1:]:
        gain = gain * one(*cut)
    return gain


def noise(key, extent, scale, most, cuts=(), held_as=jnp.bfloat16):
    values = scale * jax.random.normal(key, extent, jnp.float32)
    if cuts:
        values = values * shard_levels(key, extent, cuts, -0.22, 0.18)
    return jnp.clip(values, -most, most).astype(held_as)


def setup_inputs(seed: int = 0) -> dict:
    arg_keys = jax.random.split(jax.random.key(seed), 11)
    return {
        "tokens": draw_tokens(jax.random.fold_in(arg_keys[10], 71), 0),
        "norm_gain": jnp.clip(jnp.exp(jax.random.uniform(arg_keys[1], (D,), jnp.float32, math.log(0.5), math.log(2.0))), 0.5, 2.0),
        "w_qkv": draw_w_qkv(jax.random.fold_in(arg_keys[10], 71), 0),
        "q_gain": jnp.clip(jnp.exp(math.log(2.5) - 1.609438 * jax.random.uniform(arg_keys[3], (HEADS * HEAD_DIM,), jnp.float32) ** shard_levels(arg_keys[3], (HEADS * HEAD_DIM,), ((0, 4),), -0.2, 0.2)), 0.5, 2.5),
        "k_gain": jnp.clip(jnp.exp(math.log(2.5) - 1.609438 * jax.random.uniform(arg_keys[4], (HEADS * HEAD_DIM,), jnp.float32) ** shard_levels(arg_keys[4], (HEADS * HEAD_DIM,), ((0, 4),), -0.2, 0.2)), 0.5, 2.5),
        "w_out": noise(arg_keys[5], (HEADS * HEAD_DIM, D), (HEADS * HEAD_DIM) ** -0.5, 0.125, ((0, 4), (1, 128))),
        "grids": draw_grids(jax.random.fold_in(arg_keys[10], 71), 0),
        "owners": draw_owners(jax.random.fold_in(arg_keys[10], 71), 0),
        "proj_gain": jnp.clip(jnp.exp(math.log(2.0) - 1.3862944 * jax.random.uniform(arg_keys[8], (4, D), jnp.float32) ** shard_levels(arg_keys[8], (4, D), ((1, 4),), -0.2, 0.2)), 0.5, 2.0),
        "proj_bias": noise(arg_keys[9], (4, D), 0.5, 3.0, ((1, 4),), jnp.float32),
    }


def merge_layout(grid, token_count, slot_count):
    half_rows = grid[:, 0]
    half_cols = grid[:, 1]
    image_slots = half_rows * half_cols
    slot_ends = jnp.cumsum(image_slots).astype(jnp.int32)
    slot_starts = slot_ends - image_slots
    slot_ids = jnp.arange(slot_count, dtype=jnp.int32)
    image_ids = lax.optimization_barrier(jnp.sum((slot_ids[:, None] >= slot_ends[None, :]).astype(jnp.int32), axis=1)).astype(jnp.int32)
    image_count = grid.shape[0]
    is_live = image_ids < image_count
    one_hot = (image_ids[:, None] == jnp.arange(image_count, dtype=jnp.int32)[None, :]).astype(jnp.int32)
    cols_here = jnp.maximum(lax.optimization_barrier(jnp.sum(one_hot * half_cols[None, :], axis=1)), 1).astype(jnp.int32)
    start_here = lax.optimization_barrier(jnp.sum(one_hot * slot_starts[None, :], axis=1)).astype(jnp.int32)
    offset = slot_ids - start_here
    row_half = offset // cols_here
    col_half = offset % cols_here
    first_row = 4 * start_here + 4 * row_half * cols_here + 2 * col_half
    patch_rows = jnp.stack([first_row, first_row + 1, first_row + 2 * cols_here, first_row + 2 * cols_here + 1], axis=1)
    patch_rows = jnp.where(is_live[:, None], patch_rows, 0).astype(jnp.int32)
    token_ids = jnp.arange(token_count, dtype=jnp.int32)
    segment = lax.optimization_barrier(jnp.sum((token_ids[:, None] >= 4 * slot_ends[None, :]).astype(jnp.int32), axis=1)).astype(jnp.int32)
    return (patch_rows, is_live, segment)

def owner_ranks(owner_ids, is_live):
    slot_ids = jnp.arange(owner_ids.shape[0], dtype=jnp.int32)
    earlier = (owner_ids[:, None] == owner_ids[None, :]) & (slot_ids[None, :] < slot_ids[:, None]) & is_live[None, :]
    return lax.optimization_barrier(jnp.sum(earlier.astype(jnp.int32), axis=1)).astype(jnp.int32)

def reference(tokens, norm_gain, w_qkv, q_gain, k_gain, w_out, grids, owners, proj_gain, proj_bias):
    head_width = HEADS * HEAD_DIM
    head_share = head_width // N_TP
    score_scale = 1.0 / math.sqrt(HEAD_DIM)

    def one_device(device):
        token_rows = lax.dynamic_slice_in_dim(tokens, device * TOK_DEV, TOK_DEV, 0)
        grid = lax.dynamic_slice_in_dim(grids, device * IMG_DEV, IMG_DEV, 0)
        owner_ids = lax.dynamic_slice_in_dim(owners, device * MRG_DEV, MRG_DEV, 0)
        patch_rows, is_live, segment = merge_layout(grid, TOK_DEV, MRG_DEV)
        token_float = token_rows.astype(jnp.float32)
        mean_square = lax.optimization_barrier(jnp.mean(token_float * token_float, axis=1, keepdims=True))
        normed = (token_float * lax.rsqrt(mean_square + 1e-06) * norm_gain).astype(jnp.bfloat16)
        projected = jnp.dot(normed, w_qkv, preferred_element_type=jnp.float32).reshape(TOK_DEV, HEADS, 3, HEAD_DIM)
        queries = projected[:, :, 0]
        key_vecs = projected[:, :, 1]
        values = projected[:, :, 2].astype(jnp.bfloat16)
        q_scale = lax.rsqrt(lax.optimization_barrier(jnp.sum(queries * queries, axis=(1, 2))) / head_width + 1e-06)
        k_scale = lax.rsqrt(lax.optimization_barrier(jnp.sum(key_vecs * key_vecs, axis=(1, 2))) / head_width + 1e-06)
        q_normed = queries * q_scale[:, None, None] * q_gain.reshape(HEADS, HEAD_DIM)
        k_normed = key_vecs * k_scale[:, None, None] * k_gain.reshape(HEADS, HEAD_DIM)
        scores = jnp.einsum('qhd,khd->hqk', q_normed, k_normed, precision=lax.Precision.HIGHEST) * score_scale
        same_image = segment[:, None] == segment[None, :]
        scores = jnp.where(same_image[None], scores, -1e+30)
        row_top = lax.optimization_barrier(jnp.max(scores, axis=2, keepdims=True))
        weights_raw = jnp.exp(scores - row_top)
        probs = (weights_raw / lax.optimization_barrier(jnp.sum(weights_raw, axis=2, keepdims=True))).astype(jnp.bfloat16)
        attended = jnp.einsum('hqk,khd->qhd', probs.astype(jnp.float32), values.astype(jnp.float32))
        attended = attended.astype(jnp.bfloat16).reshape(TOK_DEV, head_width)
        summed = jnp.zeros((TOK_DEV, D), jnp.float32)
        for group in range(N_TP):
            lower = group * head_share
            partial_term = jnp.dot(attended[:, lower:lower + head_share], w_out[lower:lower + head_share], preferred_element_type=jnp.float32).astype(jnp.bfloat16)
            partial_term = lax.optimization_barrier(partial_term)
            summed = summed + partial_term.astype(jnp.float32)
        hidden = (token_float + summed).astype(jnp.bfloat16)
        merged = hidden[patch_rows].astype(jnp.float32)
        merged = jnp.where(is_live[:, None, None], merged, 0.0)
        feature_total = 4 * D
        mean_value = lax.optimization_barrier(jnp.sum(merged, axis=(1, 2))) / feature_total
        mean_sq = lax.optimization_barrier(jnp.sum(merged * merged, axis=(1, 2))) / feature_total
        variance = mean_sq - mean_value * mean_value
        normed_rows = (merged - mean_value[:, None, None]) * lax.rsqrt(variance + 1e-05)[:, None, None] * proj_gain + proj_bias
        normed_rows = jnp.where(is_live[:, None, None], normed_rows, 0.0).astype(jnp.bfloat16)
        ranks = owner_ranks(owner_ids, is_live)
        return (normed_rows, is_live, ranks, owner_ids)
    rows_all, live_all, rank_all, owner_all = lax.map(one_device, jnp.arange(N_REQ, dtype=jnp.int32))
    slot_total = N_REQ * N_REQ * CAP
    sources = jnp.arange(N_REQ, dtype=jnp.int32)[:, None]
    target = owner_all * (N_REQ * CAP) + sources * CAP + rank_all
    target = jnp.where(live_all, target, slot_total).astype(jnp.int32)
    result = jnp.zeros((slot_total, 4, D), jnp.bfloat16)
    result = result.at[target.reshape(-1)].set(rows_all.reshape(-1, 4, D), mode='drop')
    return result
```

```python
import functools
import math

import jax
import jax.numpy as jnp
from jax import lax
from jax.experimental import pallas as pl
from jax.experimental.pallas import tpu as pltpu
from jax.sharding import PartitionSpec as P

D = 3200
HEADS = 16
HEAD_DIM = 128
MESH = pl.DeviceIdType.MESH
SIDE = 8
SLAB = 400
PART = ((0, 200), (200, 200))
HALF = 104


def from_everyone(x, axis):
    copies = jnp.broadcast_to(x, (lax.axis_size(axis), *x.shape))
    return lax.all_to_all(copies, axis, split_axis=0, concat_axis=0, tiled=True)


def over_copies(x, axis):
    everything = from_everyone(x, axis)
    return jnp.sum(everything, axis=0)


def in_one(arrays, axis):
    ravelled, at, done = (jnp.concatenate([a.reshape(-1) for a in arrays]), 0, [])
    subtotal = over_copies(ravelled, axis)
    for a in arrays:
        done.append(subtotal[at : at + a.size].reshape(a.shape))
        at += a.size
    return tuple(done)


def merge_layout(grid, token_count, slot_count):
    half_rows = grid[:, 0]
    half_cols = grid[:, 1]
    image_slots = half_rows * half_cols
    slot_ends = jnp.cumsum(image_slots)
    slot_starts = slot_ends - image_slots
    slot_ids = jnp.arange(slot_count, dtype=jnp.int32)
    image_ids = jnp.sum((slot_ids[:, None] >= slot_ends[None, :]).astype(jnp.int32), axis=1)
    image_count = grid.shape[0]
    is_live = image_ids < image_count
    one_hot = (image_ids[:, None] == jnp.arange(image_count, dtype=jnp.int32)[None, :]).astype(
        jnp.int32
    )
    cols_here = jnp.maximum(jnp.sum(one_hot * half_cols[None, :], axis=1), 1)
    start_here = jnp.sum(one_hot * slot_starts[None, :], axis=1)
    offset = slot_ids - start_here
    row_half = offset // cols_here
    col_half = offset % cols_here
    first_row = 4 * start_here + 4 * row_half * cols_here + 2 * col_half
    patch_rows = jnp.stack(
        [first_row, first_row + 1, first_row + 2 * cols_here, first_row + 2 * cols_here + 1], axis=1
    )
    patch_rows = jnp.where(is_live[:, None], patch_rows, 0)
    token_ids = jnp.arange(token_count, dtype=jnp.int32)
    segment = jnp.sum((token_ids[:, None] >= 4 * slot_ends[None, :]).astype(jnp.int32), axis=1)
    return (patch_rows, is_live, segment)


def owner_ranks(owner_ids, is_live):
    slot_ids = jnp.arange(owner_ids.shape[0], dtype=jnp.int32)
    earlier = (
        (owner_ids[:, None] == owner_ids[None, :])
        & (slot_ids[None, :] < slot_ids[:, None])
        & is_live[None, :]
    )
    return jnp.sum(earlier.astype(jnp.int32), axis=1)


def shard_of(z, y, core):
    return (z * SIDE + y) * 2 + core


def gather_kernel(mine, out, own_sem, send_sem, pair_sem, r1, r2):
    me = lax.axis_index("req")
    z = me // (2 * SIDE)
    y = (me // 2) % SIDE
    core = me % 2
    partner = shard_of(z, y, 1 - core)

    def up(v, by):
        return lax.rem(v + by + SIDE, SIDE)

    def ident(part, p, q):
        return shard_of(p, q, core) if part == 0 else shard_of(q, p, core)

    where = ((z, y), (y, z))
    around = [shard_of(up(z, 1), y, core), shard_of(up(z, -1), y, core)]
    across = [shard_of(z, up(y, 1), core), shard_of(z, up(y, -1), core)]
    first = (around, across)
    second = (across, around)

    barrier = pltpu.get_barrier_semaphore()
    for other in around + across + [partner]:
        pl.semaphore_signal(barrier, inc=1, device_id={"req": other}, device_id_type=MESH)
    pl.semaphore_wait(barrier, 5)

    own = pltpu.make_async_copy(mine, out.at[me], own_sem)
    own.start()

    def piece(part, half):
        low, rows = PART[part]
        if half is None:
            return low, rows
        return (low, HALF) if half == 0 else (low + HALF, rows - HALF)

    def copy(shard, part, half, sem, to, source=None):
        low, rows = piece(part, half)
        dst = out.at[shard, pl.ds(low, rows)]
        src = dst if source is None else source.at[pl.ds(low, rows)]
        return pltpu.make_async_remote_copy(
            src_ref=src,
            dst_ref=dst,
            send_sem=send_sem,
            recv_sem=sem,
            device_id={"req": to},
            device_id_type=MESH,
        )

    def spread(part, j, shard, source=None):
        for way in range(2):
            copy(shard, part, None, r2.at[part, way, 0, j], second[part][way], source).start()
        copy(shard, part, None, pair_sem, partner, source).start()

    for part in range(2):
        for way in range(2):
            copy(me, part, None, r1.at[part, way, 0], first[part][way], mine).start()
    for part in range(2):
        spread(part, 0, me, mine)
    for k in range(1, 5):
        for part in range(2):
            p, q = where[part]
            if k < 4:
                for way in range(2):
                    shard = ident(part, up(p, -k if way == 0 else k), q)
                    copy(shard, part, None, r1.at[part, way, k - 1], partner).wait_recv()
                    half = None if k < 3 else way
                    copy(shard, part, half, r1.at[part, way, k], first[part][way]).start()
                    spread(part, 2 * k - 1 + way, shard)
            else:
                shard = ident(part, up(p, 4), q)
                for way in range(2):
                    copy(shard, part, way, r1.at[part, way, 3], partner).wait_recv()
                spread(part, 7, shard)
    for h in range(1, 5):

        def step(j, carry):
            sign = 1 - 2 * (j % 2)
            off = ((j + 1) // 2) * sign
            for part in range(2):
                p, q = where[part]
                p_here = up(p, off)
                if h < 4:
                    for way in range(2):
                        shard = ident(part, p_here, up(q, -h if way == 0 else h))
                        copy(shard, part, None, r2.at[part, way, h - 1, j], partner).wait_recv()
                        half = None if h < 3 else way
                        copy(shard, part, half, r2.at[part, way, h, j], second[part][way]).start()
                        copy(shard, part, None, pair_sem, partner).start()
                else:
                    shard = ident(part, p_here, up(q, 4))
                    for way in range(2):
                        copy(shard, part, way, r2.at[part, way, 3, j], partner).wait_recv()
                    copy(shard, part, None, pair_sem, partner).start()
            return carry

        lax.fori_loop(0, SIDE, step, 0)

    own.wait()
    half_all = out.at[pl.ds(0, 64)]
    pltpu.make_async_copy(half_all, half_all, pair_sem).wait()
    sent = out.at[pl.ds(0, 127)]
    pltpu.make_async_copy(sent, sent, send_sem).wait()


def gather_weights(slab):
    count = lax.axis_size("req")
    return pl.pallas_call(
        gather_kernel,
        out_shape=jax.ShapeDtypeStruct((count, SLAB, 128), jnp.bfloat16),
        in_specs=[pl.BlockSpec(memory_space=pl.ANY)],
        out_specs=pl.BlockSpec(memory_space=pl.ANY),
        scratch_shapes=[
            pltpu.SemaphoreType.DMA,
            pltpu.SemaphoreType.DMA,
            pltpu.SemaphoreType.DMA,
            pltpu.SemaphoreType.DMA((2, 2, 4)),
            pltpu.SemaphoreType.DMA((2, 2, 4, SIDE)),
        ],
        compiler_params=pltpu.CompilerParams(collective_id=0, has_side_effects=True),
        name="gather_weights",
    )(slab)


def norm_kernel(tokens, gain, out, normed):
    x = tokens[...].astype(jnp.float32)
    square = jnp.mean(x * x, axis=1, keepdims=True)
    normed[...] = (x * lax.rsqrt(square + 1e-06) * gain[...]).astype(jnp.bfloat16)
    for j in range(24):
        start = (128 * j + (128 * j) // 24) // 128 * 128
        width = min(384, D - start)
        source = lax.broadcasted_iota(jnp.int32, (width, 128), 0) + start
        target = lax.broadcasted_iota(jnp.int32, (width, 128), 1) + 128 * j
        pick = (source == target + target // 24).astype(jnp.bfloat16)
        out[:, 128 * j : 128 * (j + 1)] = jnp.dot(
            normed[:, start : start + width], pick, preferred_element_type=jnp.float32
        ).astype(jnp.bfloat16)
    source = lax.broadcasted_iota(jnp.int32, (D, 128), 0)
    target = lax.broadcasted_iota(jnp.int32, (D, 128), 1)
    pick = (source == target * 25 + 24).astype(jnp.bfloat16)
    out[:, 3072:] = jnp.dot(normed[...], pick, preferred_element_type=jnp.float32).astype(
        jnp.bfloat16
    )


def norm_tokens(tokens, gain):
    return pl.pallas_call(
        norm_kernel,
        out_shape=jax.ShapeDtypeStruct(tokens.shape, jnp.bfloat16),
        scratch_shapes=[pltpu.VMEM(tokens.shape, jnp.bfloat16)],
        compiler_params=pltpu.CompilerParams(vmem_limit_bytes=60 << 20),
        name="norm_tokens",
    )(tokens, gain.reshape(1, D))


def project_kernel(x, blocks, left, out):
    weight = jnp.concatenate(
        [blocks[:, :24].reshape(3072, 128), blocks[:, 24:].reshape(3072, 128)], axis=1
    )
    total = jnp.dot(x[:, :3072], weight, preferred_element_type=jnp.float32)
    total += jnp.dot(x[:, 3072:], left[...], preferred_element_type=jnp.float32)
    out[...] = total


def project(x, gathered, left):
    rows = x.shape[0]
    return pl.pallas_call(
        project_kernel,
        grid=(6,),
        out_shape=jax.ShapeDtypeStruct((rows, 1536), jnp.float32),
        in_specs=[
            pl.BlockSpec((rows, D), lambda i: (0, 0)),
            pl.BlockSpec((128, 48, 128), lambda i: (0, i, 0)),
            pl.BlockSpec((128, 256), lambda i: (0, i)),
        ],
        out_specs=pl.BlockSpec((rows, 256), lambda i: (0, i)),
        compiler_params=pltpu.CompilerParams(vmem_limit_bytes=60 << 20),
        name="project",
    )(x, gathered, left)


def body(tokens, norm_gain, w_qkv, q_gain, k_gain, w_out, grids, owners, proj_gain, proj_bias):
    token_count = tokens.shape[0]
    slot_count = owners.shape[0]
    quarter = proj_gain.shape[1]
    head_share = q_gain.shape[0]
    head_count = head_share // HEAD_DIM
    head_width = HEADS * HEAD_DIM
    score_scale = 1.0 / math.sqrt(HEAD_DIM)
    feature_total = 4 * D
    devices_req = lax.axis_size("req")
    capacity = max(2, (2 * slot_count + devices_req - 1) // devices_req)
    patch_rows, is_live, segment = merge_layout(grids, token_count, slot_count)
    token_float = tokens.astype(jnp.float32)

    both = jnp.concatenate([w_qkv, w_out.T], axis=1)
    slab = jnp.concatenate(
        [
            both[:24].reshape(24, 16, 128).transpose(1, 0, 2).reshape(384, 128),
            both[24].reshape(16, 128),
        ],
        axis=0,
    )
    gathered = gather_weights(slab)
    normed = norm_tokens(tokens, norm_gain)
    left = gathered[:, 384:, :].reshape(devices_req, 2048)
    projected = project(normed, gathered, left[:, :1536])
    out_rows = gathered[:, 288:384, :].reshape(devices_req, 4, 24, 128)
    out_left = gathered[:, 396:400, :].reshape(devices_req, 4, 1, 128)
    w_out_all = jnp.concatenate([out_rows, out_left], axis=2)

    projected = projected.reshape(token_count, head_count, 3, HEAD_DIM)
    queries = projected[:, :, 0]
    key_vecs = projected[:, :, 1]
    values = projected[:, :, 2].astype(jnp.bfloat16)
    q_gains = q_gain.reshape(head_count, HEAD_DIM)
    k_gains = k_gain.reshape(head_count, HEAD_DIM)
    local_q = jnp.sum(queries * queries, axis=(1, 2))
    local_k = jnp.sum(key_vecs * key_vecs, axis=(1, 2))
    q_total, k_total = in_one((local_q, local_k), "tp")
    q_scale = lax.rsqrt(q_total / head_width + 1e-06)
    k_scale = lax.rsqrt(k_total / head_width + 1e-06)
    q_normed = queries * q_scale[:, None, None] * q_gains
    k_normed = key_vecs * k_scale[:, None, None] * k_gains
    scores = (
        jnp.einsum("qhd,khd->hqk", q_normed, k_normed, precision=lax.Precision.HIGHEST)
        * score_scale
    )
    same_image = segment[:, None] == segment[None, :]
    scores = jnp.where(same_image[None], scores, -1e30)
    row_top = jnp.max(scores, axis=2, keepdims=True)
    weights_raw = jnp.exp(scores - row_top)
    probs = (weights_raw / jnp.sum(weights_raw, axis=2, keepdims=True)).astype(jnp.bfloat16)
    attended = jnp.einsum("hqk,khd->qhd", probs, values, preferred_element_type=jnp.float32)
    attended = attended.astype(jnp.bfloat16)
    partial_sum = jnp.einsum(
        "qhd,shrd->qsr", attended, w_out_all, preferred_element_type=jnp.float32
    ).reshape(token_count, D)
    mine = lax.psum_scatter(
        partial_sum.astype(jnp.bfloat16), "tp", scatter_dimension=1, tiled=True
    ).astype(jnp.float32)
    token_mine = lax.dynamic_slice_in_dim(token_float, lax.axis_index("tp") * quarter, quarter, 1)
    hidden = (token_mine + mine).astype(jnp.bfloat16)
    merged = jnp.where(is_live[:, None, None], hidden[patch_rows], jnp.zeros((), jnp.bfloat16))
    ranks = owner_ranks(owners, is_live)
    target_owner = jnp.where(is_live, owners, devices_req)
    merged_float = merged.astype(jnp.float32)
    row_sum = jnp.sum(merged_float, axis=(1, 2))
    row_sq = jnp.sum(merged_float * merged_float, axis=(1, 2))
    row_sum, row_sq = in_one((row_sum, row_sq), "tp")
    mean_value = row_sum / feature_total
    variance = row_sq / feature_total - mean_value * mean_value
    normed_rows = (merged_float - mean_value[:, None, None]) * lax.rsqrt(variance + 1e-05)[
        :, None, None
    ] * proj_gain + proj_bias
    normed_rows = jnp.where(is_live[:, None, None], normed_rows, 0.0).astype(jnp.bfloat16)
    send_slots = jnp.zeros((devices_req, capacity, 4, quarter), jnp.bfloat16)
    send_slots = send_slots.at[target_owner, ranks].set(normed_rows, mode="drop")
    arrived = lax.all_to_all(send_slots, "req", split_axis=0, concat_axis=0, tiled=True)
    result = arrived.reshape(devices_req * capacity, 4, quarter)
    return result


def solution(mesh):
    placed = (
        P("req", None),
        P(),
        P("req", "tp"),
        P("tp"),
        P("tp"),
        P("tp", "req"),
        P("req", None),
        P("req"),
        P(None, "tp"),
        P(None, "tp"),
    )
    return jax.shard_map(
        body, mesh=mesh, in_specs=placed, out_specs=P("req", None, "tp"), check_vma=False
    )
```

```python
import functools
import math

import jax
import jax.numpy as jnp
from jax import lax
from jax.experimental import pallas as pl
from jax.experimental.pallas import tpu as pltpu
from jax.sharding import PartitionSpec as P

D = 3200
HEADS = 16
HEAD_DIM = 128
MESH = pl.DeviceIdType.MESH
SIDE = 8
SLAB = 400
PART = ((0, 200), (200, 200))
HALF = 104
TOK = 384
SHARE = 800


def shard_of(z, y, core):
    return (z * SIDE + y) * 2 + core


def gather_kernel(mine, out, own_sem, send_sem, pair_sem, r1, r2):
    me = lax.axis_index("req")
    z = me // (2 * SIDE)
    y = (me // 2) % SIDE
    core = me % 2
    partner = shard_of(z, y, 1 - core)

    def up(v, by):
        return lax.rem(v + by + SIDE, SIDE)

    def ident(part, p, q):
        return shard_of(p, q, core) if part == 0 else shard_of(q, p, core)

    where = ((z, y), (y, z))
    around = [shard_of(up(z, 1), y, core), shard_of(up(z, -1), y, core)]
    across = [shard_of(z, up(y, 1), core), shard_of(z, up(y, -1), core)]
    first = (around, across)
    second = (across, around)

    barrier = pltpu.get_barrier_semaphore()
    for other in around + across + [partner]:
        pl.semaphore_signal(barrier, inc=1, device_id={"req": other}, device_id_type=MESH)
    pl.semaphore_wait(barrier, 5)

    own = pltpu.make_async_copy(mine, out.at[me], own_sem)
    own.start()

    def piece(part, half):
        low, rows = PART[part]
        if half is None:
            return low, rows
        return (low, HALF) if half == 0 else (low + HALF, rows - HALF)

    def copy(shard, part, half, sem, to, source=None):
        low, rows = piece(part, half)
        dst = out.at[shard, pl.ds(low, rows)]
        src = dst if source is None else source.at[pl.ds(low, rows)]
        return pltpu.make_async_remote_copy(
            src_ref=src,
            dst_ref=dst,
            send_sem=send_sem,
            recv_sem=sem,
            device_id={"req": to},
            device_id_type=MESH,
        )

    def spread(part, j, shard, source=None):
        for way in range(2):
            copy(shard, part, None, r2.at[part, way, 0, j], second[part][way], source).start()
        copy(shard, part, None, pair_sem, partner, source).start()

    for part in range(2):
        for way in range(2):
            copy(me, part, None, r1.at[part, way, 0], first[part][way], mine).start()
    for part in range(2):
        spread(part, 0, me, mine)
    for k in range(1, 5):
        for part in range(2):
            p, q = where[part]
            if k < 4:
                for way in range(2):
                    shard = ident(part, up(p, -k if way == 0 else k), q)
                    copy(shard, part, None, r1.at[part, way, k - 1], partner).wait_recv()
                    half = None if k < 3 else way
                    copy(shard, part, half, r1.at[part, way, k], first[part][way]).start()
                    spread(part, 2 * k - 1 + way, shard)
            else:
                shard = ident(part, up(p, 4), q)
                for way in range(2):
                    copy(shard, part, way, r1.at[part, way, 3], partner).wait_recv()
                spread(part, 7, shard)
    for h in range(1, 5):

        def step(j, carry):
            sign = 1 - 2 * (j % 2)
            off = ((j + 1) // 2) * sign
            for part in range(2):
                p, q = where[part]
                p_here = up(p, off)
                if h < 4:
                    for way in range(2):
                        shard = ident(part, p_here, up(q, -h if way == 0 else h))
                        copy(shard, part, None, r2.at[part, way, h - 1, j], partner).wait_recv()
                        half = None if h < 3 else way
                        copy(shard, part, half, r2.at[part, way, h, j], second[part][way]).start()
                        copy(shard, part, None, pair_sem, partner).start()
                else:
                    shard = ident(part, p_here, up(q, 4))
                    for way in range(2):
                        copy(shard, part, way, r2.at[part, way, 3, j], partner).wait_recv()
                    copy(shard, part, None, pair_sem, partner).start()
            return carry

        lax.fori_loop(0, SIDE, step, 0)

    own.wait()
    half_all = out.at[pl.ds(0, 64)]
    pltpu.make_async_copy(half_all, half_all, pair_sem).wait()
    sent = out.at[pl.ds(0, 127)]
    pltpu.make_async_copy(sent, sent, send_sem).wait()


def gather_weights(slab):
    count = lax.axis_size("req")
    return pl.pallas_call(
        gather_kernel,
        out_shape=jax.ShapeDtypeStruct((count, SLAB, 128), jnp.bfloat16),
        in_specs=[pl.BlockSpec(memory_space=pl.ANY)],
        out_specs=pl.BlockSpec(memory_space=pl.ANY),
        scratch_shapes=[
            pltpu.SemaphoreType.DMA,
            pltpu.SemaphoreType.DMA,
            pltpu.SemaphoreType.DMA,
            pltpu.SemaphoreType.DMA((2, 2, 4)),
            pltpu.SemaphoreType.DMA((2, 2, 4, SIDE)),
        ],
        compiler_params=pltpu.CompilerParams(collective_id=0, has_side_effects=True),
        name="gather_weights",
    )(slab)


def norm_kernel(tokens, gain, out, token_share, normed):
    x = tokens[...].astype(jnp.float32)
    square = jnp.mean(x * x, axis=1, keepdims=True)
    normed[...] = (x * lax.rsqrt(square + 1e-06) * gain[...]).astype(jnp.bfloat16)
    for j in range(24):
        start = (128 * j + (128 * j) // 24) // 128 * 128
        width = min(384, D - start)
        source = lax.broadcasted_iota(jnp.int32, (width, 128), 0) + start
        target = lax.broadcasted_iota(jnp.int32, (width, 128), 1) + 128 * j
        pick = (source == target + target // 24).astype(jnp.bfloat16)
        out[:, 128 * j : 128 * (j + 1)] = jnp.dot(
            normed[:, start : start + width], pick, preferred_element_type=jnp.float32
        ).astype(jnp.bfloat16)
    source = lax.broadcasted_iota(jnp.int32, (D, 128), 0)
    target = lax.broadcasted_iota(jnp.int32, (D, 128), 1)
    pick = (source == target * 25 + 24).astype(jnp.bfloat16)
    out[:, 3072:] = jnp.dot(normed[...], pick, preferred_element_type=jnp.float32).astype(
        jnp.bfloat16
    )
    tp = lax.axis_index("tp")
    window = tokens[:, pl.ds(pl.multiple_of(tp * 768, 128), 896)]
    row = lax.broadcasted_iota(jnp.int32, (SHARE, 896), 0)
    lane = lax.broadcasted_iota(jnp.int32, (SHARE, 896), 1)
    feature = jnp.where(row < 768, row + row // 24, (row - 768) * 25 + 24)
    pick = (lane == feature + 32 * tp).astype(jnp.bfloat16)
    token_share[...] = lax.dot_general(
        pick, window, (((1,), (1,)), ((), ())), preferred_element_type=jnp.float32
    ).astype(jnp.bfloat16)


def norm_tokens(tokens, gain):
    return pl.pallas_call(
        norm_kernel,
        out_shape=(
            jax.ShapeDtypeStruct(tokens.shape, jnp.bfloat16),
            jax.ShapeDtypeStruct((SHARE, tokens.shape[0]), jnp.bfloat16),
        ),
        scratch_shapes=[pltpu.VMEM(tokens.shape, jnp.bfloat16)],
        compiler_params=pltpu.CompilerParams(vmem_limit_bytes=60 << 20),
        name="norm_tokens",
    )(tokens, gain.reshape(1, D))


def as_column(row):
    n = row.shape[1]
    return jnp.transpose(jnp.broadcast_to(row, (128, n)))[:, :1]


def finish_kernel(
    x_ref, token_share, left, q_gain, k_gain, grids, owners, p_gain, p_bias, gathered,
    out,
    wq, wo_raw, wo, proj, v_t, att, own_part, hold, sums, relay_in, final_in, hidden,
    stat_mine, stat_in, row_mine, row_in, slots,
    load_sem, stat_sem, row_sem, relay_sem, final_sem, send_sem, out_sem, own_sem,
):
    me = lax.axis_index("req")
    tp = lax.axis_index("tp")
    z = me // (2 * SIDE)
    devices = lax.axis_size("req")
    right = lax.rem(tp + 1, 4)
    opposite = lax.rem(tp + 2, 4)
    left_x = lax.rem(tp + 3, 4)

    barrier = pltpu.get_barrier_semaphore()

    def greet(i, carry):
        other = lax.rem(me + i, devices)
        pl.semaphore_signal(barrier, inc=1, device_id={"req": other}, device_id_type=MESH)
        return carry

    lax.fori_loop(1, devices, greet, 0)
    for other in (right, opposite, left_x):
        pl.semaphore_signal(barrier, inc=1, device_id={"tp": other}, device_id_type=MESH)

    loads = [
        pltpu.make_async_copy(gathered.at[:, pl.ds(48 * i, 48)], wq.at[i], load_sem.at[i])
        for i in range(6)
    ]
    loads.append(pltpu.make_async_copy(gathered.at[:, pl.ds(288, 96)], wo_raw, load_sem.at[6]))
    for load in loads:
        load.start()

    def project(i, carry):
        pltpu.make_async_copy(
            gathered.at[:, pl.ds(0, 48)], wq.at[i], load_sem.at[i]
        ).wait()
        weight = jnp.concatenate(
            [wq[i, :, :24].reshape(3072, 128), wq[i, :, 24:].reshape(3072, 128)], axis=1
        )
        at = pl.multiple_of(i * 256, 256)
        total = jnp.dot(x_ref[:, :3072], weight, preferred_element_type=jnp.float32)
        total += jnp.dot(
            x_ref[:, 3072:], left[:, pl.ds(at, 256)], preferred_element_type=jnp.float32
        )
        proj[:, pl.ds(at, 256)] = total
        return carry

    lax.fori_loop(0, 6, project, 0)

    pl.semaphore_wait(barrier, devices - 1 + 3)

    def to_row(other, mine, into, sem, total_sem):
        return pltpu.make_async_remote_copy(
            src_ref=mine,
            dst_ref=into.at[tp],
            send_sem=total_sem,
            recv_sem=sem,
            device_id={"tp": other},
            device_id_type=MESH,
        )

    q_sum = jnp.zeros((TOK, 1), jnp.float32)
    k_sum = jnp.zeros((TOK, 1), jnp.float32)
    for h in range(4):
        q = proj[:, h * 384 : h * 384 + 128]
        k = proj[:, h * 384 + 128 : h * 384 + 256]
        q_sum += jnp.sum(q * q, axis=1, keepdims=True)
        k_sum += jnp.sum(k * k, axis=1, keepdims=True)
    lane = lax.broadcasted_iota(jnp.int32, (TOK, 128), 1)
    both = jnp.where(lane == 0, q_sum, jnp.where(lane == 1, k_sum, 0.0))
    stat_mine[...] = jnp.transpose(both)[:8]
    stat_in[pl.ds(tp, 1)] = stat_mine[...][None]
    stat_copies = [
        to_row(o, stat_mine, stat_in, stat_sem.at[0], stat_sem.at[1])
        for o in (opposite, right, left_x)
    ]
    for c in stat_copies:
        c.start()

    for h in range(4):
        v_t[h] = jnp.transpose(proj[:, h * 384 + 256 : h * 384 + 384]).astype(jnp.bfloat16)
    loads[6].wait()

    def pack(t, carry):
        at = pl.multiple_of(t * 32, 32)
        for b in range(4):
            block = wo_raw[pl.ds(at, 32), b * 24 : (b + 1) * 24]
            wo[t, :768, b * 128 : (b + 1) * 128] = block.reshape(768, 128)
        wo[t, 768:] = left[pl.ds(at, 32), 1536:]
        return carry

    lax.fori_loop(0, 4, pack, 0)

    ends = []
    total = 0
    for i in range(3):
        total = total + grids[i, 0] * grids[i, 1]
        ends.append(total)

    def segment(ids, scale):
        found = jnp.zeros(ids.shape, jnp.int32)
        for e in ends:
            found += (ids >= scale * e).astype(jnp.int32)
        return found

    key_segment = segment(lax.broadcasted_iota(jnp.int32, (TOK, 128), 0), 4)

    pltpu.make_async_copy(stat_in.at[pl.ds(0, 3)], stat_in.at[pl.ds(0, 3)], stat_sem.at[0]).wait()
    totals = stat_in[0] + stat_in[1] + stat_in[2] + stat_in[3]
    scales = lax.rsqrt(totals / (HEADS * HEAD_DIM) + 1e-06)
    q_scale = as_column(scales[0:1])
    k_scale = as_column(scales[1:2])
    for h in range(4):
        at = h * 384
        head = slice(h * 128, (h + 1) * 128)
        proj[:, at : at + 128] = proj[:, at : at + 128] * q_scale * q_gain[:, head]
        proj[:, at + 128 : at + 256] = proj[:, at + 128 : at + 256] * k_scale * k_gain[:, head]

    def push(source, into, sem, other):
        return pltpu.make_async_remote_copy(
            src_ref=source,
            dst_ref=into,
            send_sem=send_sem.at[0],
            recv_sem=sem,
            device_id={"tp": other},
            device_id_type=MESH,
        )

    low, high = pl.ds(0, 400), pl.ds(400, 400)

    def relay(b):
        for way, (rows, other) in enumerate(((low, right), (high, left_x))):
            push(relay_in.at[way, b], relay_in.at[way, b], relay_sem.at[way, b], other).wait_recv()
            total = hold[way, b] + relay_in[way, b].astype(jnp.float32)
            sums[1 + way, b, rows] = total.astype(jnp.bfloat16)
            push(
                sums.at[1 + way, b, rows], final_in.at[way, b, rows],
                final_sem.at[way, b, 1], other,
            ).start()

    for b in range(3):
        q_at = slice(b * 128, (b + 1) * 128)
        same = key_segment == segment(
            lax.broadcasted_iota(jnp.int32, (TOK, 128), 1) + 128 * b, 4
        )
        for h in range(4):
            at = h * 384
            scores = lax.dot_general(
                proj[:, at + 128 : at + 256],
                proj[q_at, at : at + 128],
                (((1,), (1,)), ((), ())),
                precision=lax.Precision.HIGHEST,
                preferred_element_type=jnp.float32,
            ) * (1.0 / math.sqrt(HEAD_DIM))
            scores = jnp.where(same, scores, -1e30)
            raw = jnp.exp(scores - jnp.max(scores, axis=0, keepdims=True))
            probs = (raw * (1.0 / jnp.sum(raw, axis=0, keepdims=True))).astype(jnp.bfloat16)
            att[b, h * 128 : (h + 1) * 128] = jnp.dot(
                v_t[h], probs, preferred_element_type=jnp.float32
            ).astype(jnp.bfloat16)
        attended = att[b]

        def term(t):
            return jnp.dot(wo[t], attended, preferred_element_type=jnp.float32)

        sums[0, b] = term(opposite).astype(jnp.bfloat16)
        push(sums.at[0, b, low], relay_in.at[0, b], relay_sem.at[0, b], right).start()
        push(sums.at[0, b, high], relay_in.at[1, b], relay_sem.at[1, b], left_x).start()
        to_right = term(right)
        sums[1, b, high] = to_right[400:].astype(jnp.bfloat16)
        push(
            sums.at[1, b, high], final_in.at[0, b, high], final_sem.at[0, b, 0], right
        ).start()
        hold[0, b] = to_right[:400]
        to_left = term(left_x)
        sums[2, b, low] = to_left[:400].astype(jnp.bfloat16)
        push(
            sums.at[2, b, low], final_in.at[1, b, low], final_sem.at[1, b, 0], left_x
        ).start()
        hold[1, b] = to_left[400:]
        own_part[b] = term(tp)
        if b > 0:
            relay(b - 1)
    relay(2)

    row = lax.broadcasted_iota(jnp.int32, (SHARE, SHARE), 0)
    column = lax.broadcasted_iota(jnp.int32, (SHARE, SHARE), 1)
    feature = jnp.where(column < 768, column + column // 24, (column - 768) * 25 + 24)
    unpick = (row == feature).astype(jnp.bfloat16)
    for b in range(3):
        for way, rows in ((0, (low, high)), (1, (high, low))):
            for i in range(2):
                here = final_in.at[way, b, rows[i]]
                push(here, here, final_sem.at[way, b, 1 - i], right).wait_recv()
        total = own_part[b] + final_in[0, b].astype(jnp.float32)
        total += final_in[1, b].astype(jnp.float32)
        total += token_share[:, b * 128 : (b + 1) * 128].astype(jnp.float32)
        rounded = jnp.dot(unpick, total.astype(jnp.bfloat16), preferred_element_type=jnp.float32)
        hidden[:, b * 128 : (b + 1) * 128] = rounded.astype(jnp.bfloat16)
        row_mine[0:1, b * 128 : (b + 1) * 128] = jnp.sum(rounded, axis=0, keepdims=True)
        row_mine[1:2, b * 128 : (b + 1) * 128] = jnp.sum(rounded * rounded, axis=0, keepdims=True)
    row_mine[2:] = jnp.zeros((6, TOK), jnp.float32)
    row_in[pl.ds(tp, 1)] = row_mine[...][None]
    row_copies = [
        to_row(o, row_mine, row_in, row_sem.at[0], row_sem.at[1])
        for o in (opposite, right, left_x)
    ]
    for c in row_copies:
        c.start()

    slot = lax.broadcasted_iota(jnp.int32, (1, 128), 1)
    image = segment(slot, 1)
    owner = jnp.where(image < 3, owners[...], -1)
    cols = jnp.ones((1, 128), jnp.int32)
    start = jnp.zeros((1, 128), jnp.int32)
    for i in range(3):
        cols = jnp.where(image == i, grids[i, 1], cols)
        if i:
            start = jnp.where(image == i, ends[i - 1], start)
    offset = slot - start
    row_half = jnp.zeros((1, 128), jnp.int32)
    for i in range(1, 48):
        row_half += (offset >= i * cols).astype(jnp.int32)
    first_row = 2 * start + offset + row_half * cols
    first_row = 2 * first_row
    owner_square = jnp.broadcast_to(owner, (128, 128))
    owner_down = jnp.transpose(owner_square)
    earlier = lax.broadcasted_iota(jnp.int32, (128, 128), 0) < lax.broadcasted_iota(
        jnp.int32, (128, 128), 1
    )
    rank = jnp.sum(
        jnp.where((owner_down == owner_square) & earlier, 1, 0), axis=0, keepdims=True
    )

    pltpu.make_async_copy(row_in.at[pl.ds(0, 3)], row_in.at[pl.ds(0, 3)], row_sem.at[0]).wait()
    row_total = row_in[0] + row_in[1] + row_in[2] + row_in[3]
    sum_row = row_total[0:1]
    square_row = row_total[1:2]
    gain = jnp.concatenate([p_gain[...], p_gain[...]], axis=0)[None]
    bias = jnp.concatenate([p_bias[...], p_bias[...]], axis=0)[None]

    def send_plane(i, carry):
        base = lax.rem(z + i, SIDE) * 16
        line = lax.broadcasted_iota(jnp.int32, (128, 128), 0)
        found = (owner == base + line // 8) & (rank == (line // 4) % 2)
        first = jnp.sum(jnp.where(found, first_row, 0), axis=1, keepdims=True)
        across = 2 * jnp.sum(jnp.where(found, cols, 0), axis=1, keepdims=True)
        filled = across > 0
        first = jnp.where(filled, first, -10000)
        part = lax.broadcasted_iota(jnp.int32, (128, 1), 0) % 4
        token = lax.broadcasted_iota(jnp.int32, (128, TOK), 1)
        mine = first + part % 2 + (part // 2) * across
        pick = (token == mine).astype(jnp.bfloat16)
        raw = lax.dot_general(
            pick, hidden[...], (((1,), (1,)), ((), ())), preferred_element_type=jnp.float32
        )
        upper, lower = token - first, token - first - across
        any_part = (upper == 0) | (upper == 1) | (lower == 0) | (lower == 1)
        mean = jnp.sum(jnp.where(any_part, sum_row, 0.0), axis=1, keepdims=True) / (4 * D)
        square = jnp.sum(jnp.where(any_part, square_row, 0.0), axis=1, keepdims=True) / (4 * D)
        scale = lax.rsqrt(square - mean * mean + 1e-05)
        value = ((raw - mean) * scale).reshape(16, 8, SHARE) * gain + bias
        value = jnp.where(filled, value.reshape(128, SHARE), 0.0)
        slots[pl.ds(base, 16)] = value.reshape(16, 8, SHARE).astype(jnp.bfloat16)

        def send(j, carry):
            other = base + j

            @pl.when(other != me)
            def _():
                pltpu.make_async_remote_copy(
                    src_ref=slots.at[other],
                    dst_ref=out.at[me],
                    send_sem=send_sem.at[1],
                    recv_sem=out_sem,
                    device_id={"req": other},
                    device_id_type=MESH,
                ).start()

            return carry

        lax.fori_loop(0, 16, send, 0)
        return carry

    lax.fori_loop(0, SIDE, send_plane, 0)
    keep = pltpu.make_async_copy(slots.at[me], out.at[me], own_sem)
    keep.start()
    keep.wait()
    pltpu.make_async_copy(stat_in.at[pl.ds(0, 3)], stat_in.at[pl.ds(0, 3)], stat_sem.at[1]).wait()
    pltpu.make_async_copy(row_in.at[pl.ds(0, 3)], row_in.at[pl.ds(0, 3)], row_sem.at[1]).wait()
    pltpu.make_async_copy(sums, sums, send_sem.at[0]).wait()
    most = out.at[pl.ds(0, 127)]
    pltpu.make_async_copy(most, most, send_sem.at[1]).wait()
    pltpu.make_async_copy(most, most, out_sem).wait()


def finish(x, token_share, left, q_gain, k_gain, grids, owners, p_gain, p_bias, gathered):
    vmem = pl.BlockSpec(memory_space=pltpu.VMEM)
    bf16, f32 = jnp.bfloat16, jnp.float32
    dma = pltpu.SemaphoreType.DMA
    return pl.pallas_call(
        finish_kernel,
        out_shape=jax.ShapeDtypeStruct((128, 8, SHARE), bf16),
        in_specs=[vmem] * 5
        + [pl.BlockSpec(memory_space=pltpu.SMEM)]
        + [vmem] * 3
        + [pl.BlockSpec(memory_space=pl.ANY)],
        out_specs=pl.BlockSpec(memory_space=pl.ANY),
        scratch_shapes=[
            pltpu.VMEM((6, 128, 48, 128), bf16),
            pltpu.VMEM((128, 96, 128), bf16),
            pltpu.VMEM((4, SHARE, 512), bf16),
            pltpu.VMEM((TOK, 1536), f32),
            pltpu.VMEM((4, 128, TOK), bf16),
            pltpu.VMEM((3, 512, 128), bf16),
            pltpu.VMEM((3, SHARE, 128), f32),
            pltpu.VMEM((2, 3, 400, 128), f32),
            pltpu.VMEM((3, 3, SHARE, 128), bf16),
            pltpu.VMEM((2, 3, 400, 128), bf16),
            pltpu.VMEM((2, 3, SHARE, 128), bf16),
            pltpu.VMEM((SHARE, TOK), bf16),
            pltpu.VMEM((8, TOK), f32),
            pltpu.VMEM((4, 8, TOK), f32),
            pltpu.VMEM((8, TOK), f32),
            pltpu.VMEM((4, 8, TOK), f32),
            pltpu.VMEM((128, 8, SHARE), bf16),
            dma((7,)),
            dma((2,)),
            dma((2,)),
            dma((2, 3)),
            dma((2, 3, 2)),
            dma((2,)),
            dma,
            dma,
        ],
        compiler_params=pltpu.CompilerParams(
            collective_id=1, has_side_effects=True, vmem_limit_bytes=60 << 20
        ),
        name="finish",
    )(x, token_share, left, q_gain, k_gain, grids, owners, p_gain, p_bias, gathered)


def body(tokens, norm_gain, w_qkv, q_gain, k_gain, w_out, grids, owners, proj_gain, proj_bias):
    both = jnp.concatenate([w_qkv, w_out.T], axis=1)
    slab = jnp.concatenate(
        [
            both[:24].reshape(24, 16, 128).transpose(1, 0, 2).reshape(384, 128),
            both[24].reshape(16, 128),
        ],
        axis=0,
    )
    gathered = gather_weights(slab)
    normed, token_share = norm_tokens(tokens, norm_gain)
    left = gathered[:, 384:, :].reshape(-1, 2048)
    slot_owner = jnp.pad(owners, (0, 128 - owners.shape[0]), constant_values=-1).reshape(1, 128)
    arrived = finish(
        normed, token_share, left, q_gain.reshape(1, -1), k_gain.reshape(1, -1),
        grids, slot_owner, proj_gain, proj_bias, gathered,
    )
    return arrived.reshape(-1, 4, SHARE)


def solution(mesh):
    placed = (
        P("req", None),
        P(),
        P("req", "tp"),
        P("tp"),
        P("tp"),
        P("tp", "req"),
        P("req", None),
        P("req"),
        P(None, "tp"),
        P(None, "tp"),
    )
    return jax.shard_map(
        body, mesh=mesh, in_specs=placed, out_specs=P("req", None, "tp"), check_vma=False
    )
```

```python
import functools
import math

import jax
import jax.numpy as jnp
from jax import lax
from jax.experimental import pallas as pl
from jax.experimental.pallas import tpu as pltpu
from jax.sharding import PartitionSpec as P

D = 3200
HEADS = 16
HEAD_DIM = 128
MESH = pl.DeviceIdType.MESH
SIDE = 8
SLAB = 400
PART = ((0, 200), (200, 200))
HALF = 104
TOK = 384
SHARE = 800


def shard_of(z, y, core):
    return (z * SIDE + y) * 2 + core


def gather_kernel(
    w_qkv, w_out, gain, tokens, out, permuted, token_share,
    mine, held, normed, own_sem, send_sem, pair_sem, token_sem, r1, r2,
):
    me = lax.axis_index("req")
    z = me // (2 * SIDE)
    y = (me // 2) % SIDE
    core = me % 2
    partner = shard_of(z, y, 1 - core)

    def up(v, by):
        return lax.rem(v + by + SIDE, SIDE)

    def ident(part, p, q):
        return shard_of(p, q, core) if part == 0 else shard_of(q, p, core)

    where = ((z, y), (y, z))
    around = [shard_of(up(z, 1), y, core), shard_of(up(z, -1), y, core)]
    across = [shard_of(z, up(y, 1), core), shard_of(z, up(y, -1), core)]
    first = (around, across)
    second = (across, around)

    barrier = pltpu.get_barrier_semaphore()
    for other in around + across + [partner]:
        pl.semaphore_signal(barrier, inc=1, device_id={"req": other}, device_id_type=MESH)
    token_load = pltpu.make_async_copy(tokens, held, token_sem)
    token_load.start()

    last = jnp.zeros((16, 128), jnp.float32)
    row = lax.broadcasted_iota(jnp.int32, (16, 128), 0)
    for b in range(16):
        weight, at = (w_qkv, 128 * b) if b < 12 else (w_out, 128 * (b - 12))
        mine[24 * b : 24 * b + 24] = weight[:24, at : at + 128]
        end = weight[24:25, at : at + 128].astype(jnp.float32)
        last = jnp.where(row == b, end, last)
    mine[384:400] = last.astype(jnp.bfloat16)
    pl.semaphore_wait(barrier, 5)

    own = pltpu.make_async_copy(mine, out.at[me], own_sem)
    own.start()

    def piece(part, half):
        low, rows = PART[part]
        if half is None:
            return low, rows
        return (low, HALF) if half == 0 else (low + HALF, rows - HALF)

    def copy(shard, part, half, sem, to, source=None):
        low, rows = piece(part, half)
        dst = out.at[shard, pl.ds(low, rows)]
        src = dst if source is None else source.at[pl.ds(low, rows)]
        return pltpu.make_async_remote_copy(
            src_ref=src,
            dst_ref=dst,
            send_sem=send_sem,
            recv_sem=sem,
            device_id={"req": to},
            device_id_type=MESH,
        )

    def spread(part, j, shard, source=None):
        for way in range(2):
            copy(shard, part, None, r2.at[part, way, 0, j], second[part][way], source).start()
        copy(shard, part, None, pair_sem, partner, source).start()

    for part in range(2):
        for way in range(2):
            copy(me, part, None, r1.at[part, way, 0], first[part][way], mine).start()
    for part in range(2):
        spread(part, 0, me, mine)
    token_load.wait()
    square = jnp.zeros((TOK, 128), jnp.float32)
    for j in range(25):
        x = held[:, 128 * j : 128 * (j + 1)].astype(jnp.float32)
        square += x * x
    scale = lax.rsqrt(jnp.sum(square, axis=1, keepdims=True) / D + 1e-06)
    for j in range(25):
        x = held[:, 128 * j : 128 * (j + 1)].astype(jnp.float32)
        normed[:, 128 * j : 128 * (j + 1)] = (x * scale * gain[j : j + 1]).astype(jnp.bfloat16)

    for k in range(1, 5):
        for part in range(2):
            p, q = where[part]
            if k < 4:
                for way in range(2):
                    shard = ident(part, up(p, -k if way == 0 else k), q)
                    copy(shard, part, None, r1.at[part, way, k - 1], partner).wait_recv()
                    half = None if k < 3 else way
                    copy(shard, part, half, r1.at[part, way, k], first[part][way]).start()
                    spread(part, 2 * k - 1 + way, shard)
            else:
                shard = ident(part, up(p, 4), q)
                for way in range(2):
                    copy(shard, part, way, r1.at[part, way, 3], partner).wait_recv()
                spread(part, 7, shard)
    for h in range(1, 5):

        def step(j, carry):
            sign = 1 - 2 * (j % 2)
            off = ((j + 1) // 2) * sign
            for part in range(2):
                p, q = where[part]
                p_here = up(p, off)
                if h < 4:
                    for way in range(2):
                        shard = ident(part, p_here, up(q, -h if way == 0 else h))
                        copy(shard, part, None, r2.at[part, way, h - 1, j], partner).wait_recv()
                        half = None if h < 3 else way
                        copy(shard, part, half, r2.at[part, way, h, j], second[part][way]).start()
                        copy(shard, part, None, pair_sem, partner).start()
                else:
                    shard = ident(part, p_here, up(q, 4))
                    for way in range(2):
                        copy(shard, part, way, r2.at[part, way, 3, j], partner).wait_recv()
                    copy(shard, part, None, pair_sem, partner).start()
            if h < 4:
                base = 128 * (8 * (h - 1) + j)
                start = jnp.minimum((base + base // 24) // 128 * 128, D - 384)
                start = pl.multiple_of(start, 128)
                source = lax.broadcasted_iota(jnp.int32, (384, 128), 0) + start
                target = lax.broadcasted_iota(jnp.int32, (384, 128), 1) + base
                pick = (source == target + target // 24).astype(jnp.bfloat16)
                permuted[:, pl.ds(pl.multiple_of(base, 128), 128)] = jnp.dot(
                    normed[:, pl.ds(start, 384)], pick, preferred_element_type=jnp.float32
                ).astype(jnp.bfloat16)
            return carry

        lax.fori_loop(0, SIDE, step, 0)
        if h == 2:
            source = lax.broadcasted_iota(jnp.int32, (D, 128), 0)
            target = lax.broadcasted_iota(jnp.int32, (D, 128), 1)
            pick = (source == target * 25 + 24).astype(jnp.bfloat16)
            permuted[:, 3072:] = jnp.dot(
                normed[...], pick, preferred_element_type=jnp.float32
            ).astype(jnp.bfloat16)
        if h == 3:
            tp = lax.axis_index("tp")
            window = held[:, pl.ds(pl.multiple_of(tp * 768, 128), 896)]
            row = lax.broadcasted_iota(jnp.int32, (SHARE, 896), 0)
            lane = lax.broadcasted_iota(jnp.int32, (SHARE, 896), 1)
            feature = jnp.where(row < 768, row + row // 24, (row - 768) * 25 + 24)
            pick = (lane == feature + 32 * tp).astype(jnp.bfloat16)
            token_share[...] = lax.dot_general(
                pick, window, (((1,), (1,)), ((), ())), preferred_element_type=jnp.float32
            ).astype(jnp.bfloat16)

    own.wait()
    half_all = out.at[pl.ds(0, 64)]
    pltpu.make_async_copy(half_all, half_all, pair_sem).wait()
    sent = out.at[pl.ds(0, 127)]
    pltpu.make_async_copy(sent, sent, send_sem).wait()


def gather_weights(w_qkv, w_out, gain, tokens):
    vmem, anywhere = pl.BlockSpec(memory_space=pltpu.VMEM), pl.BlockSpec(memory_space=pl.ANY)
    bf16 = jnp.bfloat16
    return pl.pallas_call(
        gather_kernel,
        out_shape=(
            jax.ShapeDtypeStruct((lax.axis_size("req"), SLAB, 128), bf16),
            jax.ShapeDtypeStruct((TOK, D), bf16),
            jax.ShapeDtypeStruct((SHARE, TOK), bf16),
        ),
        in_specs=[vmem, vmem, vmem, anywhere],
        out_specs=(anywhere, vmem, vmem),
        scratch_shapes=[
            pltpu.VMEM((SLAB, 128), bf16),
            pltpu.VMEM((TOK, D), bf16),
            pltpu.VMEM((TOK, D), bf16),
            pltpu.SemaphoreType.DMA,
            pltpu.SemaphoreType.DMA,
            pltpu.SemaphoreType.DMA,
            pltpu.SemaphoreType.DMA,
            pltpu.SemaphoreType.DMA((2, 2, 4)),
            pltpu.SemaphoreType.DMA((2, 2, 4, SIDE)),
        ],
        compiler_params=pltpu.CompilerParams(
            collective_id=0, has_side_effects=True, vmem_limit_bytes=60 << 20
        ),
        name="gather_weights",
    )(w_qkv, w_out, gain, tokens)


def as_column(row):
    n = row.shape[1]
    return jnp.transpose(jnp.broadcast_to(row, (128, n)))[:, :1]


def finish_kernel(
    x_ref, token_share, q_gain, k_gain, grids, owners, p_gain, p_bias, gathered,
    out,
    wq, wo_raw, last_raw, last_wide, left, slot_owner, wo, proj, v_t, att, own_part, hold, sums, relay_in, final_in, hidden,
    stat_mine, stat_in, row_mine, row_in, slots,
    load_sem, stat_sem, row_sem, relay_sem, final_sem, send_sem, out_sem, own_sem,
):
    me = lax.axis_index("req")
    tp = lax.axis_index("tp")
    z = me // (2 * SIDE)
    devices = lax.axis_size("req")
    right = lax.rem(tp + 1, 4)
    opposite = lax.rem(tp + 2, 4)
    left_x = lax.rem(tp + 3, 4)

    barrier = pltpu.get_barrier_semaphore()

    def greet(i, carry):
        other = lax.rem(me + i, devices)
        pl.semaphore_signal(barrier, inc=1, device_id={"req": other}, device_id_type=MESH)
        return carry

    lax.fori_loop(1, devices, greet, 0)
    for other in (right, opposite, left_x):
        pl.semaphore_signal(barrier, inc=1, device_id={"tp": other}, device_id_type=MESH)

    loads = [
        pltpu.make_async_copy(gathered.at[:, pl.ds(48 * i, 48)], wq.at[i], load_sem.at[i])
        for i in range(6)
    ]
    loads.append(pltpu.make_async_copy(gathered.at[:, pl.ds(288, 96)], wo_raw, load_sem.at[6]))
    loads.append(
        pltpu.make_async_copy(gathered.at[:, pl.ds(384, 16)], last_raw, load_sem.at[7])
    )
    for load in loads[7:] + loads[:7]:
        load.start()

    loads[7].wait()
    last_wide[...] = last_raw[...].astype(jnp.float32)
    for b in range(16):
        left[:, 128 * b : 128 * (b + 1)] = last_wide[:, b, :].astype(jnp.bfloat16)

    def project(i, carry):
        pltpu.make_async_copy(
            gathered.at[:, pl.ds(0, 48)], wq.at[i], load_sem.at[i]
        ).wait()
        weight = jnp.concatenate(
            [wq[i, :, :24].reshape(3072, 128), wq[i, :, 24:].reshape(3072, 128)], axis=1
        )
        at = pl.multiple_of(i * 256, 256)
        total = jnp.dot(x_ref[:, :3072], weight, preferred_element_type=jnp.float32)
        total += jnp.dot(
            x_ref[:, 3072:], left[:, pl.ds(at, 256)], preferred_element_type=jnp.float32
        )
        proj[:, pl.ds(at, 256)] = total
        return carry

    lax.fori_loop(0, 6, project, 0)

    pl.semaphore_wait(barrier, devices - 1 + 3)

    def to_row(other, mine, into, sem, total_sem):
        return pltpu.make_async_remote_copy(
            src_ref=mine,
            dst_ref=into.at[tp],
            send_sem=total_sem,
            recv_sem=sem,
            device_id={"tp": other},
            device_id_type=MESH,
        )

    q_sum = jnp.zeros((TOK, 1), jnp.float32)
    k_sum = jnp.zeros((TOK, 1), jnp.float32)
    for h in range(4):
        q = proj[:, h * 384 : h * 384 + 128]
        k = proj[:, h * 384 + 128 : h * 384 + 256]
        q_sum += jnp.sum(q * q, axis=1, keepdims=True)
        k_sum += jnp.sum(k * k, axis=1, keepdims=True)
    lane = lax.broadcasted_iota(jnp.int32, (TOK, 128), 1)
    both = jnp.where(lane == 0, q_sum, jnp.where(lane == 1, k_sum, 0.0))
    stat_mine[...] = jnp.transpose(both)[:8]
    stat_in[pl.ds(tp, 1)] = stat_mine[...][None]
    stat_copies = [
        to_row(o, stat_mine, stat_in, stat_sem.at[0], stat_sem.at[1])
        for o in (opposite, right, left_x)
    ]
    for c in stat_copies:
        c.start()

    for h in range(4):
        v_t[h] = jnp.transpose(proj[:, h * 384 + 256 : h * 384 + 384]).astype(jnp.bfloat16)
    loads[6].wait()

    def pack(t, carry):
        at = pl.multiple_of(t * 32, 32)
        for b in range(4):
            block = wo_raw[pl.ds(at, 32), b * 24 : (b + 1) * 24]
            wo[t, :768, b * 128 : (b + 1) * 128] = block.reshape(768, 128)
        wo[t, 768:] = left[pl.ds(at, 32), 1536:]
        return carry

    lax.fori_loop(0, 4, pack, 0)

    ends = []
    total = 0
    for i in range(3):
        total = total + grids[0, i] * grids[1, i]
        ends.append(total)

    def segment(ids, scale):
        found = jnp.zeros(ids.shape, jnp.int32)
        for e in ends:
            found += (ids >= scale * e).astype(jnp.int32)
        return found

    key_segment = segment(lax.broadcasted_iota(jnp.int32, (TOK, 128), 0), 4)

    pltpu.make_async_copy(stat_in.at[pl.ds(0, 3)], stat_in.at[pl.ds(0, 3)], stat_sem.at[0]).wait()
    totals = stat_in[0] + stat_in[1] + stat_in[2] + stat_in[3]
    scales = lax.rsqrt(totals / (HEADS * HEAD_DIM) + 1e-06)
    q_scale = as_column(scales[0:1])
    k_scale = as_column(scales[1:2])
    for h in range(4):
        at = h * 384
        head = slice(h * 128, (h + 1) * 128)
        proj[:, at : at + 128] = proj[:, at : at + 128] * q_scale * q_gain[:, head]
        proj[:, at + 128 : at + 256] = proj[:, at + 128 : at + 256] * k_scale * k_gain[:, head]

    def push(source, into, sem, other):
        return pltpu.make_async_remote_copy(
            src_ref=source,
            dst_ref=into,
            send_sem=send_sem.at[0],
            recv_sem=sem,
            device_id={"tp": other},
            device_id_type=MESH,
        )

    low, high = pl.ds(0, 400), pl.ds(400, 400)

    def relay(b):
        for way, (rows, other) in enumerate(((low, right), (high, left_x))):
            push(relay_in.at[way, b], relay_in.at[way, b], relay_sem.at[way, b], other).wait_recv()
            total = hold[way, b] + relay_in[way, b].astype(jnp.float32)
            sums[1 + way, b, rows] = total.astype(jnp.bfloat16)
            push(
                sums.at[1 + way, b, rows], final_in.at[way, b, rows],
                final_sem.at[way, b, 1], other,
            ).start()

    for b in range(3):
        q_at = slice(b * 128, (b + 1) * 128)
        same = key_segment == segment(
            lax.broadcasted_iota(jnp.int32, (TOK, 128), 1) + 128 * b, 4
        )
        for h in range(4):
            at = h * 384
            scores = lax.dot_general(
                proj[:, at + 128 : at + 256],
                proj[q_at, at : at + 128],
                (((1,), (1,)), ((), ())),
                precision=lax.Precision.HIGHEST,
                preferred_element_type=jnp.float32,
            ) * (1.0 / math.sqrt(HEAD_DIM))
            scores = jnp.where(same, scores, -1e30)
            raw = jnp.exp(scores - jnp.max(scores, axis=0, keepdims=True))
            probs = (raw * (1.0 / jnp.sum(raw, axis=0, keepdims=True))).astype(jnp.bfloat16)
            att[b, h * 128 : (h + 1) * 128] = jnp.dot(
                v_t[h], probs, preferred_element_type=jnp.float32
            ).astype(jnp.bfloat16)
        attended = att[b]

        def term(t):
            return jnp.dot(wo[t], attended, preferred_element_type=jnp.float32)

        sums[0, b] = term(opposite).astype(jnp.bfloat16)
        push(sums.at[0, b, low], relay_in.at[0, b], relay_sem.at[0, b], right).start()
        push(sums.at[0, b, high], relay_in.at[1, b], relay_sem.at[1, b], left_x).start()
        to_right = term(right)
        sums[1, b, high] = to_right[400:].astype(jnp.bfloat16)
        push(
            sums.at[1, b, high], final_in.at[0, b, high], final_sem.at[0, b, 0], right
        ).start()
        hold[0, b] = to_right[:400]
        to_left = term(left_x)
        sums[2, b, low] = to_left[:400].astype(jnp.bfloat16)
        push(
            sums.at[2, b, low], final_in.at[1, b, low], final_sem.at[1, b, 0], left_x
        ).start()
        hold[1, b] = to_left[400:]
        own_part[b] = term(tp)
        if b > 0:
            relay(b - 1)
    relay(2)

    row = lax.broadcasted_iota(jnp.int32, (SHARE, SHARE), 0)
    column = lax.broadcasted_iota(jnp.int32, (SHARE, SHARE), 1)
    feature = jnp.where(column < 768, column + column // 24, (column - 768) * 25 + 24)
    unpick = (row == feature).astype(jnp.bfloat16)
    for b in range(3):
        for way, rows in ((0, (low, high)), (1, (high, low))):
            for i in range(2):
                here = final_in.at[way, b, rows[i]]
                push(here, here, final_sem.at[way, b, 1 - i], right).wait_recv()
        total = own_part[b] + final_in[0, b].astype(jnp.float32)
        total += final_in[1, b].astype(jnp.float32)
        total += token_share[:, b * 128 : (b + 1) * 128].astype(jnp.float32)
        rounded = jnp.dot(unpick, total.astype(jnp.bfloat16), preferred_element_type=jnp.float32)
        hidden[:, b * 128 : (b + 1) * 128] = rounded.astype(jnp.bfloat16)
        row_mine[0:1, b * 128 : (b + 1) * 128] = jnp.sum(rounded, axis=0, keepdims=True)
        row_mine[1:2, b * 128 : (b + 1) * 128] = jnp.sum(rounded * rounded, axis=0, keepdims=True)
    row_mine[2:] = jnp.zeros((6, TOK), jnp.float32)
    row_in[pl.ds(tp, 1)] = row_mine[...][None]
    row_copies = [
        to_row(o, row_mine, row_in, row_sem.at[0], row_sem.at[1])
        for o in (opposite, right, left_x)
    ]
    for c in row_copies:
        c.start()

    slot = lax.broadcasted_iota(jnp.int32, (1, 128), 1)
    image = segment(slot, 1)
    slot_owner[...] = jnp.full((1, 128), -1, jnp.int32)
    slot_owner[:, : owners.shape[1]] = owners[...]
    owner = jnp.where(image < 3, slot_owner[...], -1)
    cols = jnp.ones((1, 128), jnp.int32)
    start = jnp.zeros((1, 128), jnp.int32)
    for i in range(3):
        cols = jnp.where(image == i, grids[1, i], cols)
        if i:
            start = jnp.where(image == i, ends[i - 1], start)
    offset = slot - start
    row_half = jnp.zeros((1, 128), jnp.int32)
    for i in range(1, 48):
        row_half += (offset >= i * cols).astype(jnp.int32)
    first_row = 2 * start + offset + row_half * cols
    first_row = 2 * first_row
    owner_square = jnp.broadcast_to(owner, (128, 128))
    owner_down = jnp.transpose(owner_square)
    earlier = lax.broadcasted_iota(jnp.int32, (128, 128), 0) < lax.broadcasted_iota(
        jnp.int32, (128, 128), 1
    )
    rank = jnp.sum(
        jnp.where((owner_down == owner_square) & earlier, 1, 0), axis=0, keepdims=True
    )

    pltpu.make_async_copy(row_in.at[pl.ds(0, 3)], row_in.at[pl.ds(0, 3)], row_sem.at[0]).wait()
    row_total = row_in[0] + row_in[1] + row_in[2] + row_in[3]
    sum_row = row_total[0:1]
    square_row = row_total[1:2]
    gain = jnp.concatenate([p_gain[...], p_gain[...]], axis=0)[None]
    bias = jnp.concatenate([p_bias[...], p_bias[...]], axis=0)[None]

    def alternate(i):
        return ((i + 1) // 2) * (1 - 2 * ((i + 1) % 2))

    def fill_plane(i, carry):
        base = lax.rem(z + alternate(i) + SIDE, SIDE) * 16
        line = lax.broadcasted_iota(jnp.int32, (128, 128), 0)
        found = (owner == base + line // 8) & (rank == (line // 4) % 2)
        first = jnp.sum(jnp.where(found, first_row, 0), axis=1, keepdims=True)
        across = 2 * jnp.sum(jnp.where(found, cols, 0), axis=1, keepdims=True)
        filled = across > 0
        first = jnp.where(filled, first, -10000)
        part = lax.broadcasted_iota(jnp.int32, (128, 1), 0) % 4
        token = lax.broadcasted_iota(jnp.int32, (128, TOK), 1)
        mine = first + part % 2 + (part // 2) * across
        pick = (token == mine).astype(jnp.bfloat16)
        raw = lax.dot_general(
            pick, hidden[...], (((1,), (1,)), ((), ())), preferred_element_type=jnp.float32
        )
        upper, lower = token - first, token - first - across
        any_part = (upper == 0) | (upper == 1) | (lower == 0) | (lower == 1)
        mean = jnp.sum(jnp.where(any_part, sum_row, 0.0), axis=1, keepdims=True) / (4 * D)
        square = jnp.sum(jnp.where(any_part, square_row, 0.0), axis=1, keepdims=True) / (4 * D)
        scale = lax.rsqrt(square - mean * mean + 1e-05)
        value = ((raw - mean) * scale).reshape(16, 8, SHARE) * gain + bias
        value = jnp.where(filled, value.reshape(128, SHARE), 0.0)
        slots[pl.ds(base, 16)] = value.reshape(16, 8, SHARE).astype(jnp.bfloat16)
        return carry

    y = (me // 2) % SIDE
    core = me % 2

    def send(i, carry):
        to_z = lax.rem(z + alternate(4 * (i // 32) + (i % 8 + (i // 8) % 4) % 4) + SIDE, SIDE)
        to_y = lax.rem(y + alternate(i % 8) + SIDE, SIDE)
        for flip in range(2):
            other = shard_of(to_z, to_y, lax.rem(core + flip, 2))

            @pl.when(other != me)
            def _():
                pltpu.make_async_remote_copy(
                    src_ref=slots.at[other],
                    dst_ref=out.at[me],
                    send_sem=send_sem.at[1],
                    recv_sem=out_sem,
                    device_id={"req": other},
                    device_id_type=MESH,
                ).start()

        return carry

    for half in range(2):
        lax.fori_loop(4 * half, 4 * half + 4, fill_plane, 0)
        lax.fori_loop(32 * half, 32 * half + 32, send, 0)
    keep = pltpu.make_async_copy(slots.at[me], out.at[me], own_sem)
    keep.start()
    keep.wait()
    pltpu.make_async_copy(stat_in.at[pl.ds(0, 3)], stat_in.at[pl.ds(0, 3)], stat_sem.at[1]).wait()
    pltpu.make_async_copy(row_in.at[pl.ds(0, 3)], row_in.at[pl.ds(0, 3)], row_sem.at[1]).wait()
    pltpu.make_async_copy(sums, sums, send_sem.at[0]).wait()
    most = out.at[pl.ds(0, 127)]
    pltpu.make_async_copy(most, most, send_sem.at[1]).wait()
    pltpu.make_async_copy(most, most, out_sem).wait()


def finish(x, token_share, q_gain, k_gain, grids, owners, p_gain, p_bias, gathered):
    vmem = pl.BlockSpec(memory_space=pltpu.VMEM)
    bf16, f32 = jnp.bfloat16, jnp.float32
    dma = pltpu.SemaphoreType.DMA
    return pl.pallas_call(
        finish_kernel,
        out_shape=jax.ShapeDtypeStruct((128, 8, SHARE), bf16),
        in_specs=[vmem] * 4
        + [pl.BlockSpec(memory_space=pltpu.SMEM)]
        + [vmem] * 3
        + [pl.BlockSpec(memory_space=pl.ANY)],
        out_specs=pl.BlockSpec(memory_space=pl.ANY),
        scratch_shapes=[
            pltpu.VMEM((6, 128, 48, 128), bf16),
            pltpu.VMEM((128, 96, 128), bf16),
            pltpu.VMEM((128, 16, 128), bf16),
            pltpu.VMEM((128, 16, 128), f32),
            pltpu.VMEM((128, 2048), bf16),
            pltpu.VMEM((1, 128), jnp.int32),
            pltpu.VMEM((4, SHARE, 512), bf16),
            pltpu.VMEM((TOK, 1536), f32),
            pltpu.VMEM((4, 128, TOK), bf16),
            pltpu.VMEM((3, 512, 128), bf16),
            pltpu.VMEM((3, SHARE, 128), f32),
            pltpu.VMEM((2, 3, 400, 128), f32),
            pltpu.VMEM((3, 3, SHARE, 128), bf16),
            pltpu.VMEM((2, 3, 400, 128), bf16),
            pltpu.VMEM((2, 3, SHARE, 128), bf16),
            pltpu.VMEM((SHARE, TOK), bf16),
            pltpu.VMEM((8, TOK), f32),
            pltpu.VMEM((4, 8, TOK), f32),
            pltpu.VMEM((8, TOK), f32),
            pltpu.VMEM((4, 8, TOK), f32),
            pltpu.VMEM((128, 8, SHARE), bf16),
            dma((8,)),
            dma((2,)),
            dma((2,)),
            dma((2, 3)),
            dma((2, 3, 2)),
            dma((2,)),
            dma,
            dma,
        ],
        compiler_params=pltpu.CompilerParams(
            collective_id=1, has_side_effects=True, vmem_limit_bytes=60 << 20
        ),
        name="finish",
    )(x, token_share, q_gain, k_gain, grids, owners, p_gain, p_bias, gathered)


def body(tokens, norm_gain, w_qkv, q_gain, k_gain, w_out, grids, owners, proj_gain, proj_bias):
    gathered, normed, token_share = gather_weights(
        w_qkv, w_out.T, norm_gain.reshape(-1, 128), tokens
    )
    arrived = finish(
        normed, token_share, q_gain.reshape(1, -1), k_gain.reshape(1, -1),
        grids.T, owners.reshape(1, -1), proj_gain, proj_bias, gathered,
    )
    return arrived.reshape(-1, 4, SHARE)


def solution(mesh):
    placed = (
        P("req", None),
        P(),
        P("req", "tp"),
        P("tp"),
        P("tp"),
        P("tp", "req"),
        P("req", None),
        P("req"),
        P(None, "tp"),
        P(None, "tp"),
    )
    return jax.shard_map(
        body, mesh=mesh, in_specs=placed, out_specs=P("req", None, "tp"), check_vma=False
    )
```

```python
import functools
import math

import jax
import jax.numpy as jnp
from jax import lax
from jax.experimental import pallas as pl
from jax.experimental.pallas import tpu as pltpu
from jax.sharding import PartitionSpec as P

D = 3200
HEADS = 16
HEAD_DIM = 128
MESH = pl.DeviceIdType.MESH
SIDE = 8
SLAB = 400
PART = ((0, 200), (200, 200))
HALF = 104
TOK = 384
SHARE = 800


def shard_of(z, y, core):
    return (z * SIDE + y) * 2 + core


def gather_kernel(
    w_qkv, w_out, gain, tokens, out, permuted, token_share,
    mine, held, normed, own_sem, send_sem, pair_sem, token_sem, r1, r2,
):
    me = lax.axis_index("req")
    z = me // (2 * SIDE)
    y = (me // 2) % SIDE
    core = me % 2
    partner = shard_of(z, y, 1 - core)

    def up(v, by):
        return lax.rem(v + by + SIDE, SIDE)

    def ident(part, p, q):
        return shard_of(p, q, core) if part == 0 else shard_of(q, p, core)

    where = ((z, y), (y, z))
    around = [shard_of(up(z, 1), y, core), shard_of(up(z, -1), y, core)]
    across = [shard_of(z, up(y, 1), core), shard_of(z, up(y, -1), core)]
    first = (around, across)
    second = (across, around)

    barrier = pltpu.get_barrier_semaphore()
    for other in around + across + [partner]:
        pl.semaphore_signal(barrier, inc=1, device_id={"req": other}, device_id_type=MESH)
    token_load = pltpu.make_async_copy(tokens, held, token_sem)
    token_load.start()

    last = jnp.zeros((16, 128), jnp.float32)
    row = lax.broadcasted_iota(jnp.int32, (16, 128), 0)
    for b in range(16):
        weight, at = (w_qkv, 128 * b) if b < 12 else (w_out, 128 * (b - 12))
        mine[24 * b : 24 * b + 24] = weight[:24, at : at + 128]
        end = weight[24:25, at : at + 128].astype(jnp.float32)
        last = jnp.where(row == b, end, last)
    mine[384:400] = last.astype(jnp.bfloat16)
    pl.semaphore_wait(barrier, 5)

    own = pltpu.make_async_copy(mine, out.at[me], own_sem)
    own.start()

    def piece(part, half):
        low, rows = PART[part]
        if half is None:
            return low, rows
        return (low, HALF) if half == 0 else (low + HALF, rows - HALF)

    def copy(shard, part, half, sem, to, source=None):
        low, rows = piece(part, half)
        dst = out.at[shard, pl.ds(low, rows)]
        src = dst if source is None else source.at[pl.ds(low, rows)]
        return pltpu.make_async_remote_copy(
            src_ref=src,
            dst_ref=dst,
            send_sem=send_sem,
            recv_sem=sem,
            device_id={"req": to},
            device_id_type=MESH,
        )

    def spread(part, j, shard, source=None):
        for way in range(2):
            copy(shard, part, None, r2.at[part, way, 0, j], second[part][way], source).start()
        copy(shard, part, None, pair_sem, partner, source).start()

    for part in range(2):
        for way in range(2):
            copy(me, part, None, r1.at[part, way, 0], first[part][way], mine).start()
    for part in range(2):
        spread(part, 0, me, mine)
    token_load.wait()
    square = jnp.zeros((TOK, 128), jnp.float32)
    for j in range(25):
        x = held[:, 128 * j : 128 * (j + 1)].astype(jnp.float32)
        square += x * x
    scale = lax.rsqrt(jnp.sum(square, axis=1, keepdims=True) / D + 1e-06)
    for j in range(25):
        x = held[:, 128 * j : 128 * (j + 1)].astype(jnp.float32)
        normed[:, 128 * j : 128 * (j + 1)] = (x * scale * gain[j : j + 1]).astype(jnp.bfloat16)

    for k in range(1, 5):
        for part in range(2):
            p, q = where[part]
            if k < 4:
                for way in range(2):
                    shard = ident(part, up(p, -k if way == 0 else k), q)
                    copy(shard, part, None, r1.at[part, way, k - 1], partner).wait_recv()
                    half = None if k < 3 else way
                    copy(shard, part, half, r1.at[part, way, k], first[part][way]).start()
                    spread(part, 2 * k - 1 + way, shard)
            else:
                shard = ident(part, up(p, 4), q)
                for way in range(2):
                    copy(shard, part, way, r1.at[part, way, 3], partner).wait_recv()
                spread(part, 7, shard)
    for h in range(1, 5):

        def step(j, carry):
            sign = 1 - 2 * (j % 2)
            off = ((j + 1) // 2) * sign
            for part in range(2):
                p, q = where[part]
                p_here = up(p, off)
                if h < 4:
                    for way in range(2):
                        shard = ident(part, p_here, up(q, -h if way == 0 else h))
                        copy(shard, part, None, r2.at[part, way, h - 1, j], partner).wait_recv()
                        half = None if h < 3 else way
                        copy(shard, part, half, r2.at[part, way, h, j], second[part][way]).start()
                        copy(shard, part, None, pair_sem, partner).start()
                else:
                    shard = ident(part, p_here, up(q, 4))
                    for way in range(2):
                        copy(shard, part, way, r2.at[part, way, 3, j], partner).wait_recv()
                    copy(shard, part, None, pair_sem, partner).start()
            if h < 4:
                base = 128 * (8 * (h - 1) + j)
                start = jnp.minimum((base + base // 24) // 128 * 128, D - 384)
                start = pl.multiple_of(start, 128)
                source = lax.broadcasted_iota(jnp.int32, (384, 128), 0) + start
                target = lax.broadcasted_iota(jnp.int32, (384, 128), 1) + base
                pick = (source == target + target // 24).astype(jnp.bfloat16)
                permuted[:, pl.ds(pl.multiple_of(base, 128), 128)] = jnp.dot(
                    normed[:, pl.ds(start, 384)], pick, preferred_element_type=jnp.float32
                ).astype(jnp.bfloat16)
            return carry

        lax.fori_loop(0, SIDE, step, 0)
        if h == 2:
            source = lax.broadcasted_iota(jnp.int32, (D, 128), 0)
            target = lax.broadcasted_iota(jnp.int32, (D, 128), 1)
            pick = (source == target * 25 + 24).astype(jnp.bfloat16)
            permuted[:, 3072:] = jnp.dot(
                normed[...], pick, preferred_element_type=jnp.float32
            ).astype(jnp.bfloat16)
        if h == 3:
            tp = lax.axis_index("tp")
            window = held[:, pl.ds(pl.multiple_of(tp * 768, 128), 896)]
            row = lax.broadcasted_iota(jnp.int32, (SHARE, 896), 0)
            lane = lax.broadcasted_iota(jnp.int32, (SHARE, 896), 1)
            feature = jnp.where(row < 768, row + row // 24, (row - 768) * 25 + 24)
            pick = (lane == feature + 32 * tp).astype(jnp.bfloat16)
            token_share[...] = lax.dot_general(
                pick, window, (((1,), (1,)), ((), ())), preferred_element_type=jnp.float32
            ).astype(jnp.bfloat16)

    own.wait()
    half_all = out.at[pl.ds(0, 64)]
    pltpu.make_async_copy(half_all, half_all, pair_sem).wait()
    sent = out.at[pl.ds(0, 127)]
    pltpu.make_async_copy(sent, sent, send_sem).wait()


def gather_weights(w_qkv, w_out, gain, tokens):
    vmem, anywhere = pl.BlockSpec(memory_space=pltpu.VMEM), pl.BlockSpec(memory_space=pl.ANY)
    bf16 = jnp.bfloat16
    return pl.pallas_call(
        gather_kernel,
        out_shape=(
            jax.ShapeDtypeStruct((lax.axis_size("req"), SLAB, 128), bf16),
            jax.ShapeDtypeStruct((TOK, D), bf16),
            jax.ShapeDtypeStruct((SHARE, TOK), bf16),
        ),
        in_specs=[vmem, vmem, vmem, anywhere],
        out_specs=(anywhere, vmem, vmem),
        scratch_shapes=[
            pltpu.VMEM((SLAB, 128), bf16),
            pltpu.VMEM((TOK, D), bf16),
            pltpu.VMEM((TOK, D), bf16),
            pltpu.SemaphoreType.DMA,
            pltpu.SemaphoreType.DMA,
            pltpu.SemaphoreType.DMA,
            pltpu.SemaphoreType.DMA,
            pltpu.SemaphoreType.DMA((2, 2, 4)),
            pltpu.SemaphoreType.DMA((2, 2, 4, SIDE)),
        ],
        compiler_params=pltpu.CompilerParams(
            collective_id=0, has_side_effects=True, vmem_limit_bytes=60 << 20
        ),
        name="gather_weights",
    )(w_qkv, w_out, gain, tokens)


def as_column(row):
    n = row.shape[1]
    return jnp.transpose(jnp.broadcast_to(row, (128, n)))[:, :1]


def finish_kernel(
    x_ref, token_share, q_gain, k_gain, grids, owners, p_gain, p_bias, gathered,
    out,
    wq, wo_raw, last_raw, last_wide, left, slot_owner, wo, proj, v_t, att, own_part, hold, sums, relay_in, final_in, hidden,
    stat_mine, stat_in, row_mine, row_in, slots,
    load_sem, stat_sem, row_sem, relay_sem, final_sem, send_sem, out_sem, own_sem,
):
    me = lax.axis_index("req")
    tp = lax.axis_index("tp")
    z = me // (2 * SIDE)
    devices = lax.axis_size("req")
    right = lax.rem(tp + 1, 4)
    opposite = lax.rem(tp + 2, 4)
    left_x = lax.rem(tp + 3, 4)

    barrier = pltpu.get_barrier_semaphore()

    def greet(i, carry):
        other = lax.rem(me + i, devices)
        pl.semaphore_signal(barrier, inc=1, device_id={"req": other}, device_id_type=MESH)
        return carry

    lax.fori_loop(1, devices, greet, 0)
    for other in (right, opposite, left_x):
        pl.semaphore_signal(barrier, inc=1, device_id={"tp": other}, device_id_type=MESH)

    loads = [
        pltpu.make_async_copy(gathered.at[:, pl.ds(48 * i, 48)], wq.at[i], load_sem.at[i])
        for i in range(6)
    ]
    loads.append(pltpu.make_async_copy(gathered.at[:, pl.ds(288, 96)], wo_raw, load_sem.at[6]))
    loads.append(
        pltpu.make_async_copy(gathered.at[:, pl.ds(384, 16)], last_raw, load_sem.at[7])
    )
    for load in loads[7:] + loads[:7]:
        load.start()

    loads[7].wait()
    last_wide[...] = last_raw[...].astype(jnp.float32)
    for b in range(16):
        left[:, 128 * b : 128 * (b + 1)] = last_wide[:, b, :].astype(jnp.bfloat16)

    def project(i, carry):
        pltpu.make_async_copy(
            gathered.at[:, pl.ds(0, 48)], wq.at[i], load_sem.at[i]
        ).wait()
        weight = jnp.concatenate(
            [wq[i, :, :24].reshape(3072, 128), wq[i, :, 24:].reshape(3072, 128)], axis=1
        )
        at = pl.multiple_of(i * 256, 256)
        total = jnp.dot(x_ref[:, :3072], weight, preferred_element_type=jnp.float32)
        total += jnp.dot(
            x_ref[:, 3072:], left[:, pl.ds(at, 256)], preferred_element_type=jnp.float32
        )
        proj[:, pl.ds(at, 256)] = total
        return carry

    lax.fori_loop(0, 6, project, 0)

    pl.semaphore_wait(barrier, devices - 1 + 3)

    def to_row(other, mine, into, sem, total_sem):
        return pltpu.make_async_remote_copy(
            src_ref=mine,
            dst_ref=into.at[tp],
            send_sem=total_sem,
            recv_sem=sem,
            device_id={"tp": other},
            device_id_type=MESH,
        )

    q_sum = jnp.zeros((TOK, 1), jnp.float32)
    k_sum = jnp.zeros((TOK, 1), jnp.float32)
    for h in range(4):
        q = proj[:, h * 384 : h * 384 + 128]
        k = proj[:, h * 384 + 128 : h * 384 + 256]
        q_sum += jnp.sum(q * q, axis=1, keepdims=True)
        k_sum += jnp.sum(k * k, axis=1, keepdims=True)
    lane = lax.broadcasted_iota(jnp.int32, (TOK, 128), 1)
    both = jnp.where(lane == 0, q_sum, jnp.where(lane == 1, k_sum, 0.0))
    stat_mine[...] = jnp.transpose(both)[:8]
    stat_in[pl.ds(tp, 1)] = stat_mine[...][None]
    stat_copies = [
        to_row(o, stat_mine, stat_in, stat_sem.at[0], stat_sem.at[1])
        for o in (opposite, right, left_x)
    ]
    for c in stat_copies:
        c.start()

    for h in range(4):
        v_t[h] = jnp.transpose(proj[:, h * 384 + 256 : h * 384 + 384]).astype(jnp.bfloat16)
    loads[6].wait()

    def pack(t, carry):
        at = pl.multiple_of(t * 32, 32)
        for b in range(4):
            block = wo_raw[pl.ds(at, 32), b * 24 : (b + 1) * 24]
            wo[t, :768, b * 128 : (b + 1) * 128] = block.reshape(768, 128)
        wo[t, 768:] = left[pl.ds(at, 32), 1536:]
        return carry

    lax.fori_loop(0, 4, pack, 0)

    ends = []
    total = 0
    for i in range(3):
        total = total + grids[0, i] * grids[1, i]
        ends.append(total)

    def segment(ids, scale):
        found = jnp.zeros(ids.shape, jnp.int32)
        for e in ends:
            found += (ids >= scale * e).astype(jnp.int32)
        return found

    key_segment = segment(lax.broadcasted_iota(jnp.int32, (TOK, 128), 0), 4)

    pltpu.make_async_copy(stat_in.at[pl.ds(0, 3)], stat_in.at[pl.ds(0, 3)], stat_sem.at[0]).wait()
    totals = stat_in[0] + stat_in[1] + stat_in[2] + stat_in[3]
    scales = lax.rsqrt(totals / (HEADS * HEAD_DIM) + 1e-06)
    q_scale = as_column(scales[0:1])
    k_scale = as_column(scales[1:2])
    for h in range(4):
        at = h * 384
        head = slice(h * 128, (h + 1) * 128)
        proj[:, at : at + 128] = proj[:, at : at + 128] * q_scale * q_gain[:, head]
        proj[:, at + 128 : at + 256] = proj[:, at + 128 : at + 256] * k_scale * k_gain[:, head]

    def push(source, into, sem, other):
        return pltpu.make_async_remote_copy(
            src_ref=source,
            dst_ref=into,
            send_sem=send_sem.at[0],
            recv_sem=sem,
            device_id={"tp": other},
            device_id_type=MESH,
        )

    low, high = pl.ds(0, 400), pl.ds(400, 400)

    def relay(b):
        for way, (rows, other) in enumerate(((low, right), (high, left_x))):
            push(relay_in.at[way, b], relay_in.at[way, b], relay_sem.at[way, b], other).wait_recv()
            total = hold[way, b] + relay_in[way, b].astype(jnp.float32)
            sums[1 + way, b, rows] = total.astype(jnp.bfloat16)
            push(
                sums.at[1 + way, b, rows], final_in.at[way, b, rows],
                final_sem.at[way, b, 1], other,
            ).start()

    for b in range(3):
        q_at = slice(b * 128, (b + 1) * 128)
        same = key_segment == segment(
            lax.broadcasted_iota(jnp.int32, (TOK, 128), 1) + 128 * b, 4
        )
        for h in range(4):
            at = h * 384
            scores = lax.dot_general(
                proj[:, at + 128 : at + 256],
                proj[q_at, at : at + 128],
                (((1,), (1,)), ((), ())),
                precision=lax.Precision.HIGHEST,
                preferred_element_type=jnp.float32,
            ) * (1.0 / math.sqrt(HEAD_DIM))
            scores = jnp.where(same, scores, -1e30)
            raw = jnp.exp(scores - jnp.max(scores, axis=0, keepdims=True))
            probs = (raw * (1.0 / jnp.sum(raw, axis=0, keepdims=True))).astype(jnp.bfloat16)
            att[b, h * 128 : (h + 1) * 128] = jnp.dot(
                v_t[h], probs, preferred_element_type=jnp.float32
            ).astype(jnp.bfloat16)
        attended = att[b]

        def term(t):
            return jnp.dot(wo[t], attended, preferred_element_type=jnp.float32)

        sums[0, b] = term(opposite).astype(jnp.bfloat16)
        push(sums.at[0, b, low], relay_in.at[0, b], relay_sem.at[0, b], right).start()
        push(sums.at[0, b, high], relay_in.at[1, b], relay_sem.at[1, b], left_x).start()
        to_right = term(right)
        sums[1, b, high] = to_right[400:].astype(jnp.bfloat16)
        push(
            sums.at[1, b, high], final_in.at[0, b, high], final_sem.at[0, b, 0], right
        ).start()
        hold[0, b] = to_right[:400]
        to_left = term(left_x)
        sums[2, b, low] = to_left[:400].astype(jnp.bfloat16)
        push(
            sums.at[2, b, low], final_in.at[1, b, low], final_sem.at[1, b, 0], left_x
        ).start()
        hold[1, b] = to_left[400:]
        own_part[b] = term(tp)
        if b > 0:
            relay(b - 1)
    relay(2)

    row = lax.broadcasted_iota(jnp.int32, (SHARE, SHARE), 0)
    column = lax.broadcasted_iota(jnp.int32, (SHARE, SHARE), 1)
    feature = jnp.where(column < 768, column + column // 24, (column - 768) * 25 + 24)
    unpick = (row == feature).astype(jnp.bfloat16)
    for b in range(3):
        for way, rows in ((0, (low, high)), (1, (high, low))):
            for i in range(2):
                here = final_in.at[way, b, rows[i]]
                push(here, here, final_sem.at[way, b, 1 - i], right).wait_recv()
        total = own_part[b] + final_in[0, b].astype(jnp.float32)
        total += final_in[1, b].astype(jnp.float32)
        total += token_share[:, b * 128 : (b + 1) * 128].astype(jnp.float32)
        rounded = jnp.dot(unpick, total.astype(jnp.bfloat16), preferred_element_type=jnp.float32)
        hidden[:, b * 128 : (b + 1) * 128] = rounded.astype(jnp.bfloat16)
        row_mine[0:1, b * 128 : (b + 1) * 128] = jnp.sum(rounded, axis=0, keepdims=True)
        row_mine[1:2, b * 128 : (b + 1) * 128] = jnp.sum(rounded * rounded, axis=0, keepdims=True)
    row_mine[2:] = jnp.zeros((6, TOK), jnp.float32)
    row_in[pl.ds(tp, 1)] = row_mine[...][None]
    row_copies = [
        to_row(o, row_mine, row_in, row_sem.at[0], row_sem.at[1])
        for o in (opposite, right, left_x)
    ]
    for c in row_copies:
        c.start()

    slot = lax.broadcasted_iota(jnp.int32, (1, 128), 1)
    image = segment(slot, 1)
    slot_owner[...] = jnp.full((1, 128), -1, jnp.int32)
    slot_owner[:, : owners.shape[1]] = owners[...]
    owner = jnp.where(image < 3, slot_owner[...], -1)
    cols = jnp.ones((1, 128), jnp.int32)
    start = jnp.zeros((1, 128), jnp.int32)
    for i in range(3):
        cols = jnp.where(image == i, grids[1, i], cols)
        if i:
            start = jnp.where(image == i, ends[i - 1], start)
    offset = slot - start
    row_half = jnp.zeros((1, 128), jnp.int32)
    for i in range(1, 48):
        row_half += (offset >= i * cols).astype(jnp.int32)
    first_row = 2 * start + offset + row_half * cols
    first_row = 2 * first_row
    owner_square = jnp.broadcast_to(owner, (128, 128))
    owner_down = jnp.transpose(owner_square)
    earlier = lax.broadcasted_iota(jnp.int32, (128, 128), 0) < lax.broadcasted_iota(
        jnp.int32, (128, 128), 1
    )
    rank = jnp.sum(
        jnp.where((owner_down == owner_square) & earlier, 1, 0), axis=0, keepdims=True
    )

    pltpu.make_async_copy(row_in.at[pl.ds(0, 3)], row_in.at[pl.ds(0, 3)], row_sem.at[0]).wait()
    row_total = row_in[0] + row_in[1] + row_in[2] + row_in[3]
    sum_row = row_total[0:1]
    square_row = row_total[1:2]
    gain = jnp.concatenate([p_gain[...], p_gain[...]], axis=0)[None]
    bias = jnp.concatenate([p_bias[...], p_bias[...]], axis=0)[None]

    def alternate(i):
        return ((i + 1) // 2) * (1 - 2 * ((i + 1) % 2))

    def fill_plane(i, carry):
        base = 16 * i
        line = lax.broadcasted_iota(jnp.int32, (128, 128), 0)
        found = (owner == base + line // 8) & (rank == (line // 4) % 2)
        first = jnp.sum(jnp.where(found, first_row, 0), axis=1, keepdims=True)
        across = 2 * jnp.sum(jnp.where(found, cols, 0), axis=1, keepdims=True)
        filled = across > 0
        first = jnp.where(filled, first, -10000)
        part = lax.broadcasted_iota(jnp.int32, (128, 1), 0) % 4
        token = lax.broadcasted_iota(jnp.int32, (128, TOK), 1)
        mine = first + part % 2 + (part // 2) * across
        pick = (token == mine).astype(jnp.bfloat16)
        raw = lax.dot_general(
            pick, hidden[...], (((1,), (1,)), ((), ())), preferred_element_type=jnp.float32
        )
        upper, lower = token - first, token - first - across
        any_part = (upper == 0) | (upper == 1) | (lower == 0) | (lower == 1)
        mean = jnp.sum(jnp.where(any_part, sum_row, 0.0), axis=1, keepdims=True) / (4 * D)
        square = jnp.sum(jnp.where(any_part, square_row, 0.0), axis=1, keepdims=True) / (4 * D)
        scale = lax.rsqrt(square - mean * mean + 1e-05)
        value = ((raw - mean) * scale).reshape(16, 8, SHARE) * gain + bias
        value = jnp.where(filled, value.reshape(128, SHARE), 0.0)
        slots[pl.ds(base, 16)] = value.reshape(16, 2, 4, SHARE).astype(jnp.bfloat16)
        return carry

    y = (me // 2) % SIDE
    core = me % 2

    def send(i, carry):
        to_z = lax.rem(z + alternate((15 - i % 8 - i // 8) % 8) + SIDE, SIDE)
        to_y = lax.rem(y + alternate(7 - i % 8) + SIDE, SIDE)
        for flip in range(2):
            other = shard_of(to_z, to_y, lax.rem(core + flip, 2))

            @pl.when(other != me)
            def _():
                pltpu.make_async_remote_copy(
                    src_ref=slots.at[other],
                    dst_ref=out.at[me],
                    send_sem=send_sem.at[1],
                    recv_sem=out_sem,
                    device_id={"req": other},
                    device_id_type=MESH,
                ).start()

        return carry

    lax.fori_loop(0, SIDE, fill_plane, 0)
    lax.fori_loop(0, SIDE * SIDE, send, 0)
    keep = pltpu.make_async_copy(slots.at[me], out.at[me], own_sem)
    keep.start()
    keep.wait()
    pltpu.make_async_copy(stat_in.at[pl.ds(0, 3)], stat_in.at[pl.ds(0, 3)], stat_sem.at[1]).wait()
    pltpu.make_async_copy(row_in.at[pl.ds(0, 3)], row_in.at[pl.ds(0, 3)], row_sem.at[1]).wait()
    pltpu.make_async_copy(sums, sums, send_sem.at[0]).wait()
    most = out.at[pl.ds(0, 127)]
    pltpu.make_async_copy(most, most, send_sem.at[1]).wait()
    pltpu.make_async_copy(most, most, out_sem).wait()


def finish(x, token_share, q_gain, k_gain, grids, owners, p_gain, p_bias, gathered):
    vmem = pl.BlockSpec(memory_space=pltpu.VMEM)
    bf16, f32 = jnp.bfloat16, jnp.float32
    dma = pltpu.SemaphoreType.DMA
    return pl.pallas_call(
        finish_kernel,
        out_shape=jax.ShapeDtypeStruct((128, 2, 4, SHARE), bf16),
        in_specs=[vmem] * 4
        + [pl.BlockSpec(memory_space=pltpu.SMEM)]
        + [vmem] * 3
        + [pl.BlockSpec(memory_space=pl.ANY)],
        out_specs=pl.BlockSpec(memory_space=pl.ANY),
        scratch_shapes=[
            pltpu.VMEM((6, 128, 48, 128), bf16),
            pltpu.VMEM((128, 96, 128), bf16),
            pltpu.VMEM((128, 16, 128), bf16),
            pltpu.VMEM((128, 16, 128), f32),
            pltpu.VMEM((128, 2048), bf16),
            pltpu.VMEM((1, 128), jnp.int32),
            pltpu.VMEM((4, SHARE, 512), bf16),
            pltpu.VMEM((TOK, 1536), f32),
            pltpu.VMEM((4, 128, TOK), bf16),
            pltpu.VMEM((3, 512, 128), bf16),
            pltpu.VMEM((3, SHARE, 128), f32),
            pltpu.VMEM((2, 3, 400, 128), f32),
            pltpu.VMEM((3, 3, SHARE, 128), bf16),
            pltpu.VMEM((2, 3, 400, 128), bf16),
            pltpu.VMEM((2, 3, SHARE, 128), bf16),
            pltpu.VMEM((SHARE, TOK), bf16),
            pltpu.VMEM((8, TOK), f32),
            pltpu.VMEM((4, 8, TOK), f32),
            pltpu.VMEM((8, TOK), f32),
            pltpu.VMEM((4, 8, TOK), f32),
            pltpu.VMEM((128, 2, 4, SHARE), bf16),
            dma((8,)),
            dma((2,)),
            dma((2,)),
            dma((2, 3)),
            dma((2, 3, 2)),
            dma((2,)),
            dma,
            dma,
        ],
        compiler_params=pltpu.CompilerParams(
            collective_id=1, has_side_effects=True, vmem_limit_bytes=60 << 20
        ),
        name="finish",
    )(x, token_share, q_gain, k_gain, grids, owners, p_gain, p_bias, gathered)


def body(tokens, norm_gain, w_qkv, q_gain, k_gain, w_out, grids, owners, proj_gain, proj_bias):
    gathered, normed, token_share = gather_weights(
        w_qkv, w_out.T, norm_gain.reshape(-1, 128), tokens
    )
    arrived = finish(
        normed, token_share, q_gain.reshape(1, -1), k_gain.reshape(1, -1),
        grids.T, owners.reshape(1, -1), proj_gain, proj_bias, gathered,
    )
    return arrived.reshape(-1, 4, SHARE)


def solution(mesh):
    placed = (
        P("req", None),
        P(),
        P("req", "tp"),
        P("tp"),
        P("tp"),
        P("tp", "req"),
        P("req", None),
        P("req"),
        P(None, "tp"),
        P(None, "tp"),
    )
    return jax.shard_map(
        body, mesh=mesh, in_specs=placed, out_specs=P("req", None, "tp"), check_vma=False
    )
```

```python
import functools
import math

import jax
import jax.numpy as jnp
from jax import lax
from jax.experimental import pallas as pl
from jax.experimental.pallas import tpu as pltpu
from jax.sharding import PartitionSpec as P

D = 3200
HEADS = 16
HEAD_DIM = 128
MESH = pl.DeviceIdType.MESH
SIDE = 8
SLAB = 400
BLOCKS = (0, 1, 3, 4, 6, 7, 9, 10, 2, 5, 8, 11)
PART = ((0, 200), (200, 200))
HALF = 104
TOK = 384
SHARE = 800


def shard_of(z, y, core):
    return (z * SIDE + y) * 2 + core


def gather_kernel(
    w_qkv, w_out, gain, tokens, out, permuted, token_share,
    mine, held, normed, own_sem, send_sem, pair_sem, token_sem, r1, r2,
):
    me = lax.axis_index("req")
    z = me // (2 * SIDE)
    y = (me // 2) % SIDE
    core = me % 2
    partner = shard_of(z, y, 1 - core)

    def up(v, by):
        return lax.rem(v + by + SIDE, SIDE)

    def ident(part, p, q):
        return shard_of(p, q, core) if part == 0 else shard_of(q, p, core)

    where = ((z, y), (y, z))
    around = [shard_of(up(z, 1), y, core), shard_of(up(z, -1), y, core)]
    across = [shard_of(z, up(y, 1), core), shard_of(z, up(y, -1), core)]
    first = (around, across)
    second = (across, around)

    barrier = pltpu.get_barrier_semaphore()
    for other in around + across + [partner]:
        pl.semaphore_signal(barrier, inc=1, device_id={"req": other}, device_id_type=MESH)
    token_load = pltpu.make_async_copy(tokens, held, token_sem)
    token_load.start()

    last = jnp.zeros((16, 128), jnp.float32)
    row = lax.broadcasted_iota(jnp.int32, (16, 128), 0)
    for b in range(16):
        weight, at = (w_qkv, 128 * BLOCKS[b]) if b < 12 else (w_out, 128 * (b - 12))
        mine[24 * b : 24 * b + 24] = weight[:24, at : at + 128]
        end = weight[24:25, at : at + 128].astype(jnp.float32)
        last = jnp.where(row == b, end, last)
    mine[384:400] = last.astype(jnp.bfloat16)
    pl.semaphore_wait(barrier, 5)

    own = pltpu.make_async_copy(mine, out.at[me], own_sem)
    own.start()

    def piece(part, half):
        low, rows = PART[part]
        if half is None:
            return low, rows
        return (low, HALF) if half == 0 else (low + HALF, rows - HALF)

    def copy(shard, part, half, sem, to, source=None):
        low, rows = piece(part, half)
        dst = out.at[shard, pl.ds(low, rows)]
        src = dst if source is None else source.at[pl.ds(low, rows)]
        return pltpu.make_async_remote_copy(
            src_ref=src,
            dst_ref=dst,
            send_sem=send_sem,
            recv_sem=sem,
            device_id={"req": to},
            device_id_type=MESH,
        )

    def spread(part, j, shard, source=None):
        for way in range(2):
            copy(shard, part, None, r2.at[part, way, 0, j], second[part][way], source).start()
        copy(shard, part, None, pair_sem, partner, source).start()

    for part in range(2):
        for way in range(2):
            copy(me, part, None, r1.at[part, way, 0], first[part][way], mine).start()
    for part in range(2):
        spread(part, 0, me, mine)
    for k in range(1, 5):
        for part in range(2):
            p, q = where[part]
            if k < 4:
                for way in range(2):
                    shard = ident(part, up(p, -k if way == 0 else k), q)
                    copy(shard, part, None, r1.at[part, way, k - 1], partner).wait_recv()
                    half = None if k < 3 else way
                    copy(shard, part, half, r1.at[part, way, k], first[part][way]).start()
                    spread(part, 2 * k - 1 + way, shard)
            else:
                shard = ident(part, up(p, 4), q)
                for way in range(2):
                    copy(shard, part, way, r1.at[part, way, 3], partner).wait_recv()
                spread(part, 7, shard)
    token_load.wait()
    square = jnp.zeros((TOK, 128), jnp.float32)
    for j in range(25):
        x = held[:, 128 * j : 128 * (j + 1)].astype(jnp.float32)
        square += x * x
    scale = lax.rsqrt(jnp.sum(square, axis=1, keepdims=True) / D + 1e-06)
    for j in range(25):
        x = held[:, 128 * j : 128 * (j + 1)].astype(jnp.float32)
        normed[:, 128 * j : 128 * (j + 1)] = (x * scale * gain[j : j + 1]).astype(jnp.bfloat16)

    for h in range(1, 5):

        def step(j, carry):
            sign = 1 - 2 * (j % 2)
            off = ((j + 1) // 2) * sign
            for part in range(2):
                p, q = where[part]
                p_here = up(p, off)
                if h < 4:
                    for way in range(2):
                        shard = ident(part, p_here, up(q, -h if way == 0 else h))
                        copy(shard, part, None, r2.at[part, way, h - 1, j], partner).wait_recv()
                        half = None if h < 3 else way
                        copy(shard, part, half, r2.at[part, way, h, j], second[part][way]).start()
                        copy(shard, part, None, pair_sem, partner).start()
                else:
                    shard = ident(part, p_here, up(q, 4))
                    for way in range(2):
                        copy(shard, part, way, r2.at[part, way, 3, j], partner).wait_recv()
                    copy(shard, part, None, pair_sem, partner).start()
            if h < 4:
                base = 128 * (8 * (h - 1) + j)
                start = jnp.minimum((base + base // 24) // 128 * 128, D - 384)
                start = pl.multiple_of(start, 128)
                source = lax.broadcasted_iota(jnp.int32, (384, 128), 0) + start
                target = lax.broadcasted_iota(jnp.int32, (384, 128), 1) + base
                pick = (source == target + target // 24).astype(jnp.bfloat16)
                permuted[:, pl.ds(pl.multiple_of(base, 128), 128)] = jnp.dot(
                    normed[:, pl.ds(start, 384)], pick, preferred_element_type=jnp.float32
                ).astype(jnp.bfloat16)
            return carry

        lax.fori_loop(0, SIDE, step, 0)
        if h == 2:
            source = lax.broadcasted_iota(jnp.int32, (D, 128), 0)
            target = lax.broadcasted_iota(jnp.int32, (D, 128), 1)
            pick = (source == target * 25 + 24).astype(jnp.bfloat16)
            permuted[:, 3072:] = jnp.dot(
                normed[...], pick, preferred_element_type=jnp.float32
            ).astype(jnp.bfloat16)
        if h == 3:
            tp = lax.axis_index("tp")
            window = held[:, pl.ds(pl.multiple_of(tp * 768, 128), 896)]
            row = lax.broadcasted_iota(jnp.int32, (SHARE, 896), 0)
            lane = lax.broadcasted_iota(jnp.int32, (SHARE, 896), 1)
            feature = jnp.where(row < 768, row + row // 24, (row - 768) * 25 + 24)
            pick = (lane == feature + 32 * tp).astype(jnp.bfloat16)
            token_share[...] = lax.dot_general(
                pick, window, (((1,), (1,)), ((), ())), preferred_element_type=jnp.float32
            ).astype(jnp.bfloat16)

    own.wait()
    half_all = out.at[pl.ds(0, 64)]
    pltpu.make_async_copy(half_all, half_all, pair_sem).wait()
    sent = out.at[pl.ds(0, 127)]
    pltpu.make_async_copy(sent, sent, send_sem).wait()


def gather_weights(w_qkv, w_out, gain, tokens):
    vmem, anywhere = pl.BlockSpec(memory_space=pltpu.VMEM), pl.BlockSpec(memory_space=pl.ANY)
    bf16 = jnp.bfloat16
    return pl.pallas_call(
        gather_kernel,
        out_shape=(
            jax.ShapeDtypeStruct((lax.axis_size("req"), SLAB, 128), bf16),
            jax.ShapeDtypeStruct((TOK, D), bf16),
            jax.ShapeDtypeStruct((SHARE, TOK), bf16),
        ),
        in_specs=[vmem, vmem, vmem, anywhere],
        out_specs=(anywhere, vmem, vmem),
        scratch_shapes=[
            pltpu.VMEM((SLAB, 128), bf16),
            pltpu.VMEM((TOK, D), bf16),
            pltpu.VMEM((TOK, D), bf16),
            pltpu.SemaphoreType.DMA,
            pltpu.SemaphoreType.DMA,
            pltpu.SemaphoreType.DMA,
            pltpu.SemaphoreType.DMA,
            pltpu.SemaphoreType.DMA((2, 2, 4)),
            pltpu.SemaphoreType.DMA((2, 2, 4, SIDE)),
        ],
        compiler_params=pltpu.CompilerParams(
            collective_id=0, has_side_effects=True, vmem_limit_bytes=60 << 20
        ),
        name="gather_weights",
    )(w_qkv, w_out, gain, tokens)


def as_column(row):
    n = row.shape[1]
    return jnp.transpose(jnp.broadcast_to(row, (128, n)))[:, :1]


def finish_kernel(
    x_ref, token_share, q_gain, k_gain, grids, owners, p_gain, p_bias, gathered,
    out,
    wq, wo_raw, last_raw, last_wide, left, slot_owner, wo, proj, v_t, att, own_part, hold, sums, relay_in, final_in, hidden,
    stat_mine, stat_in, row_mine, row_in, picks, members, raws, slots,
    load_sem, stat_sem, row_sem, relay_sem, final_sem, send_sem, out_sem, own_sem,
):
    me = lax.axis_index("req")
    tp = lax.axis_index("tp")
    z = me // (2 * SIDE)
    devices = lax.axis_size("req")
    right = lax.rem(tp + 1, 4)
    opposite = lax.rem(tp + 2, 4)
    left_x = lax.rem(tp + 3, 4)

    barrier = pltpu.get_barrier_semaphore()

    def greet(i, carry):
        other = lax.rem(me + i, devices)
        pl.semaphore_signal(barrier, inc=1, device_id={"req": other}, device_id_type=MESH)
        return carry

    lax.fori_loop(1, devices, greet, 0)
    for other in (right, opposite, left_x):
        pl.semaphore_signal(barrier, inc=1, device_id={"tp": other}, device_id_type=MESH)

    loads = [
        pltpu.make_async_copy(gathered.at[:, pl.ds(48 * i, 48)], wq.at[i], load_sem.at[i])
        for i in range(6)
    ]
    loads.append(pltpu.make_async_copy(gathered.at[:, pl.ds(288, 96)], wo_raw, load_sem.at[6]))
    loads.append(
        pltpu.make_async_copy(gathered.at[:, pl.ds(384, 16)], last_raw, load_sem.at[7])
    )
    for load in loads[7:] + loads[:7]:
        load.start()

    loads[7].wait()
    last_wide[...] = last_raw[...].astype(jnp.float32)
    for b in range(16):
        left[:, 128 * b : 128 * (b + 1)] = last_wide[:, b, :].astype(jnp.bfloat16)

    def project(i, carry):
        pltpu.make_async_copy(
            gathered.at[:, pl.ds(0, 48)], wq.at[i], load_sem.at[i]
        ).wait()
        weight = jnp.concatenate(
            [wq[i, :, :24].reshape(3072, 128), wq[i, :, 24:].reshape(3072, 128)], axis=1
        )
        at = pl.multiple_of(i * 256, 256)
        total = jnp.dot(x_ref[:, :3072], weight, preferred_element_type=jnp.float32)
        total += jnp.dot(
            x_ref[:, 3072:], left[:, pl.ds(at, 256)], preferred_element_type=jnp.float32
        )
        proj[:, pl.ds(at, 256)] = total
        return carry

    lax.fori_loop(0, 4, project, 0)

    pl.semaphore_wait(barrier, devices - 1 + 3)

    def to_row(other, mine, into, sem, total_sem):
        return pltpu.make_async_remote_copy(
            src_ref=mine,
            dst_ref=into.at[tp],
            send_sem=total_sem,
            recv_sem=sem,
            device_id={"tp": other},
            device_id_type=MESH,
        )

    q_sum = jnp.zeros((TOK, 1), jnp.float32)
    k_sum = jnp.zeros((TOK, 1), jnp.float32)
    for h in range(4):
        q = proj[:, h * 256 : h * 256 + 128]
        k = proj[:, h * 256 + 128 : h * 256 + 256]
        q_sum += jnp.sum(q * q, axis=1, keepdims=True)
        k_sum += jnp.sum(k * k, axis=1, keepdims=True)
    lane = lax.broadcasted_iota(jnp.int32, (TOK, 128), 1)
    both = jnp.where(lane == 0, q_sum, jnp.where(lane == 1, k_sum, 0.0))
    stat_mine[...] = jnp.transpose(both)[:8]
    stat_in[pl.ds(tp, 1)] = stat_mine[...][None]
    stat_copies = [
        to_row(o, stat_mine, stat_in, stat_sem.at[0], stat_sem.at[1])
        for o in (opposite, right, left_x)
    ]
    for c in stat_copies:
        c.start()

    lax.fori_loop(4, 6, project, 0)
    for h in range(4):
        v_t[h] = jnp.transpose(proj[:, 1024 + h * 128 : 1152 + h * 128]).astype(jnp.bfloat16)
    loads[6].wait()

    def pack(t, carry):
        at = pl.multiple_of(t * 32, 32)
        for b in range(4):
            block = wo_raw[pl.ds(at, 32), b * 24 : (b + 1) * 24]
            wo[t, :768, b * 128 : (b + 1) * 128] = block.reshape(768, 128)
        wo[t, 768:] = left[pl.ds(at, 32), 1536:]
        return carry

    lax.fori_loop(0, 4, pack, 0)

    ends = []
    total = 0
    for i in range(3):
        total = total + grids[0, i] * grids[1, i]
        ends.append(total)

    def segment(ids, scale):
        found = jnp.zeros(ids.shape, jnp.int32)
        for e in ends:
            found += (ids >= scale * e).astype(jnp.int32)
        return found

    key_segment = segment(lax.broadcasted_iota(jnp.int32, (TOK, 128), 0), 4)

    pltpu.make_async_copy(stat_in.at[pl.ds(0, 3)], stat_in.at[pl.ds(0, 3)], stat_sem.at[0]).wait()
    totals = stat_in[0] + stat_in[1] + stat_in[2] + stat_in[3]
    scales = lax.rsqrt(totals / (HEADS * HEAD_DIM) + 1e-06)
    q_scale = as_column(scales[0:1])
    k_scale = as_column(scales[1:2])
    for h in range(4):
        at = h * 256
        head = slice(h * 128, (h + 1) * 128)
        proj[:, at : at + 128] = proj[:, at : at + 128] * q_scale * q_gain[:, head]
        proj[:, at + 128 : at + 256] = proj[:, at + 128 : at + 256] * k_scale * k_gain[:, head]

    def push(source, into, sem, other):
        return pltpu.make_async_remote_copy(
            src_ref=source,
            dst_ref=into,
            send_sem=send_sem.at[0],
            recv_sem=sem,
            device_id={"tp": other},
            device_id_type=MESH,
        )

    low, high = pl.ds(0, 400), pl.ds(400, 400)

    def relay(b):
        for way, (rows, other) in enumerate(((low, right), (high, left_x))):
            push(relay_in.at[way, b], relay_in.at[way, b], relay_sem.at[way, b], other).wait_recv()
            total = hold[way, b] + relay_in[way, b].astype(jnp.float32)
            sums[1 + way, b, rows] = total.astype(jnp.bfloat16)
            push(
                sums.at[1 + way, b, rows], final_in.at[way, b, rows],
                final_sem.at[way, b, 1], other,
            ).start()

    for b in range(3):
        q_at = slice(b * 128, (b + 1) * 128)
        same = key_segment == segment(
            lax.broadcasted_iota(jnp.int32, (TOK, 128), 1) + 128 * b, 4
        )
        for h in range(4):
            at = h * 256
            scores = lax.dot_general(
                proj[:, at + 128 : at + 256],
                proj[q_at, at : at + 128],
                (((1,), (1,)), ((), ())),
                precision=lax.Precision.HIGHEST,
                preferred_element_type=jnp.float32,
            ) * (1.0 / math.sqrt(HEAD_DIM))
            scores = jnp.where(same, scores, -1e30)
            raw = jnp.exp(scores - jnp.max(scores, axis=0, keepdims=True))
            probs = (raw * (1.0 / jnp.sum(raw, axis=0, keepdims=True))).astype(jnp.bfloat16)
            att[b, h * 128 : (h + 1) * 128] = jnp.dot(
                v_t[h], probs, preferred_element_type=jnp.float32
            ).astype(jnp.bfloat16)
        attended = att[b]

        def term(t):
            return jnp.dot(wo[t], attended, preferred_element_type=jnp.float32)

        sums[0, b] = term(opposite).astype(jnp.bfloat16)
        push(sums.at[0, b, low], relay_in.at[0, b], relay_sem.at[0, b], right).start()
        push(sums.at[0, b, high], relay_in.at[1, b], relay_sem.at[1, b], left_x).start()
        to_right = term(right)
        sums[1, b, high] = to_right[400:].astype(jnp.bfloat16)
        push(
            sums.at[1, b, high], final_in.at[0, b, high], final_sem.at[0, b, 0], right
        ).start()
        hold[0, b] = to_right[:400]
        to_left = term(left_x)
        sums[2, b, low] = to_left[:400].astype(jnp.bfloat16)
        push(
            sums.at[2, b, low], final_in.at[1, b, low], final_sem.at[1, b, 0], left_x
        ).start()
        hold[1, b] = to_left[400:]
        own_part[b] = term(tp)
        if b > 0:
            relay(b - 1)
    relay(2)

    slot = lax.broadcasted_iota(jnp.int32, (1, 128), 1)
    image = segment(slot, 1)
    slot_owner[...] = jnp.full((1, 128), -1, jnp.int32)
    slot_owner[:, : owners.shape[1]] = owners[...]
    owner = jnp.where(image < 3, slot_owner[...], -1)
    cols = jnp.ones((1, 128), jnp.int32)
    start = jnp.zeros((1, 128), jnp.int32)
    for i in range(3):
        cols = jnp.where(image == i, grids[1, i], cols)
        if i:
            start = jnp.where(image == i, ends[i - 1], start)
    offset = slot - start
    row_half = jnp.zeros((1, 128), jnp.int32)
    for i in range(1, 48):
        row_half += (offset >= i * cols).astype(jnp.int32)
    first_row = 2 * start + offset + row_half * cols
    first_row = 2 * first_row
    owner_square = jnp.broadcast_to(owner, (128, 128))
    owner_down = jnp.transpose(owner_square)
    earlier = lax.broadcasted_iota(jnp.int32, (128, 128), 0) < lax.broadcasted_iota(
        jnp.int32, (128, 128), 1
    )
    rank = jnp.sum(
        jnp.where((owner_down == owner_square) & earlier, 1, 0), axis=0, keepdims=True
    )

    def table(i, carry):
        base = 16 * i
        line = lax.broadcasted_iota(jnp.int32, (128, 128), 0)
        found = (owner == base + line // 8) & (rank == (line // 4) % 2)
        first = jnp.sum(jnp.where(found, first_row, 0), axis=1, keepdims=True)
        across = 2 * jnp.sum(jnp.where(found, cols, 0), axis=1, keepdims=True)
        filled = across > 0
        first = jnp.where(filled, first, -10000)
        part = lax.broadcasted_iota(jnp.int32, (128, 1), 0) % 4
        token = lax.broadcasted_iota(jnp.int32, (128, TOK), 1)
        mine = first + part % 2 + (part // 2) * across
        picks[i] = (token == mine).astype(jnp.bfloat16)
        upper, lower = token - first, token - first - across
        any_part = (upper == 0) | (upper == 1) | (lower == 0) | (lower == 1)
        members[i] = any_part.astype(jnp.float32)
        return carry

    lax.fori_loop(0, SIDE, table, 0)

    row = lax.broadcasted_iota(jnp.int32, (SHARE, SHARE), 0)
    column = lax.broadcasted_iota(jnp.int32, (SHARE, SHARE), 1)
    feature = jnp.where(column < 768, column + column // 24, (column - 768) * 25 + 24)
    unpick = (row == feature).astype(jnp.bfloat16)
    for b in range(3):
        for way, rows in ((0, (low, high)), (1, (high, low))):
            for i in range(2):
                here = final_in.at[way, b, rows[i]]
                push(here, here, final_sem.at[way, b, 1 - i], right).wait_recv()
        total = own_part[b] + final_in[0, b].astype(jnp.float32)
        total += final_in[1, b].astype(jnp.float32)
        total += token_share[:, b * 128 : (b + 1) * 128].astype(jnp.float32)
        rounded = jnp.dot(unpick, total.astype(jnp.bfloat16), preferred_element_type=jnp.float32)
        hidden[:, b * 128 : (b + 1) * 128] = rounded.astype(jnp.bfloat16)
        row_mine[0:1, b * 128 : (b + 1) * 128] = jnp.sum(rounded, axis=0, keepdims=True)
        row_mine[1:2, b * 128 : (b + 1) * 128] = jnp.sum(rounded * rounded, axis=0, keepdims=True)
    row_mine[2:] = jnp.zeros((6, TOK), jnp.float32)
    row_in[pl.ds(tp, 1)] = row_mine[...][None]
    row_copies = [
        to_row(o, row_mine, row_in, row_sem.at[0], row_sem.at[1])
        for o in (opposite, right, left_x)
    ]
    for c in row_copies:
        c.start()

    def gather_rows(i, carry):
        raws[i] = lax.dot_general(
            picks[i], hidden[...], (((1,), (1,)), ((), ())), preferred_element_type=jnp.float32
        )
        return carry

    lax.fori_loop(0, SIDE, gather_rows, 0)

    pltpu.make_async_copy(row_in.at[pl.ds(0, 3)], row_in.at[pl.ds(0, 3)], row_sem.at[0]).wait()
    row_total = row_in[0] + row_in[1] + row_in[2] + row_in[3]
    sum_row = row_total[0:1]
    square_row = row_total[1:2]
    gain = jnp.concatenate([p_gain[...], p_gain[...]], axis=0)[None]
    bias = jnp.concatenate([p_bias[...], p_bias[...]], axis=0)[None]

    def alternate(i):
        return ((i + 1) // 2) * (1 - 2 * ((i + 1) % 2))

    def fill_plane(i, carry):
        member = members[i]
        mean = jnp.sum(member * sum_row, axis=1, keepdims=True) / (4 * D)
        square = jnp.sum(member * square_row, axis=1, keepdims=True) / (4 * D)
        filled = jnp.sum(member, axis=1, keepdims=True) > 0.5
        scale = lax.rsqrt(square - mean * mean + 1e-05)
        value = ((raws[i] - mean) * scale).reshape(16, 8, SHARE) * gain + bias
        value = jnp.where(filled, value.reshape(128, SHARE), 0.0)
        slots[pl.ds(16 * i, 16)] = value.reshape(16, 2, 4, SHARE).astype(jnp.bfloat16)
        return carry

    y = (me // 2) % SIDE
    core = me % 2

    def send(i, carry):
        to_z = lax.rem(z + alternate((15 - i % 8 - i // 8) % 8) + SIDE, SIDE)
        to_y = lax.rem(y + alternate(7 - i % 8) + SIDE, SIDE)
        for flip in range(2):
            other = shard_of(to_z, to_y, lax.rem(core + flip, 2))

            @pl.when(other != me)
            def _():
                pltpu.make_async_remote_copy(
                    src_ref=slots.at[other],
                    dst_ref=out.at[me],
                    send_sem=send_sem.at[1],
                    recv_sem=out_sem,
                    device_id={"req": other},
                    device_id_type=MESH,
                ).start()

        return carry

    lax.fori_loop(0, SIDE, fill_plane, 0)
    lax.fori_loop(0, SIDE * SIDE, send, 0)
    keep = pltpu.make_async_copy(slots.at[me], out.at[me], own_sem)
    keep.start()
    keep.wait()
    pltpu.make_async_copy(stat_in.at[pl.ds(0, 3)], stat_in.at[pl.ds(0, 3)], stat_sem.at[1]).wait()
    pltpu.make_async_copy(row_in.at[pl.ds(0, 3)], row_in.at[pl.ds(0, 3)], row_sem.at[1]).wait()
    pltpu.make_async_copy(sums, sums, send_sem.at[0]).wait()
    most = out.at[pl.ds(0, 127)]
    pltpu.make_async_copy(most, most, send_sem.at[1]).wait()
    pltpu.make_async_copy(most, most, out_sem).wait()


def finish(x, token_share, q_gain, k_gain, grids, owners, p_gain, p_bias, gathered):
    vmem = pl.BlockSpec(memory_space=pltpu.VMEM)
    bf16, f32 = jnp.bfloat16, jnp.float32
    dma = pltpu.SemaphoreType.DMA
    return pl.pallas_call(
        finish_kernel,
        out_shape=jax.ShapeDtypeStruct((128, 2, 4, SHARE), bf16),
        in_specs=[vmem] * 4
        + [pl.BlockSpec(memory_space=pltpu.SMEM)]
        + [vmem] * 3
        + [pl.BlockSpec(memory_space=pl.ANY)],
        out_specs=pl.BlockSpec(memory_space=pl.ANY),
        scratch_shapes=[
            pltpu.VMEM((6, 128, 48, 128), bf16),
            pltpu.VMEM((128, 96, 128), bf16),
            pltpu.VMEM((128, 16, 128), bf16),
            pltpu.VMEM((128, 16, 128), f32),
            pltpu.VMEM((128, 2048), bf16),
            pltpu.VMEM((1, 128), jnp.int32),
            pltpu.VMEM((4, SHARE, 512), bf16),
            pltpu.VMEM((TOK, 1536), f32),
            pltpu.VMEM((4, 128, TOK), bf16),
            pltpu.VMEM((3, 512, 128), bf16),
            pltpu.VMEM((3, SHARE, 128), f32),
            pltpu.VMEM((2, 3, 400, 128), f32),
            pltpu.VMEM((3, 3, SHARE, 128), bf16),
            pltpu.VMEM((2, 3, 400, 128), bf16),
            pltpu.VMEM((2, 3, SHARE, 128), bf16),
            pltpu.VMEM((SHARE, TOK), bf16),
            pltpu.VMEM((8, TOK), f32),
            pltpu.VMEM((4, 8, TOK), f32),
            pltpu.VMEM((8, TOK), f32),
            pltpu.VMEM((4, 8, TOK), f32),
            pltpu.VMEM((SIDE, 128, TOK), bf16),
            pltpu.VMEM((SIDE, 128, TOK), f32),
            pltpu.VMEM((SIDE, 128, SHARE), f32),
            pltpu.VMEM((128, 2, 4, SHARE), bf16),
            dma((8,)),
            dma((2,)),
            dma((2,)),
            dma((2, 3)),
            dma((2, 3, 2)),
            dma((2,)),
            dma,
            dma,
        ],
        compiler_params=pltpu.CompilerParams(
            collective_id=1, has_side_effects=True, vmem_limit_bytes=60 << 20
        ),
        name="finish",
    )(x, token_share, q_gain, k_gain, grids, owners, p_gain, p_bias, gathered)


def body(tokens, norm_gain, w_qkv, q_gain, k_gain, w_out, grids, owners, proj_gain, proj_bias):
    gathered, normed, token_share = gather_weights(
        w_qkv, w_out.T, norm_gain.reshape(-1, 128), tokens
    )
    arrived = finish(
        normed, token_share, q_gain.reshape(1, -1), k_gain.reshape(1, -1),
        grids.T, owners.reshape(1, -1), proj_gain, proj_bias, gathered,
    )
    return arrived.reshape(-1, 4, SHARE)


def solution(mesh):
    placed = (
        P("req", None),
        P(),
        P("req", "tp"),
        P("tp"),
        P("tp"),
        P("tp", "req"),
        P("req", None),
        P("req"),
        P(None, "tp"),
        P(None, "tp"),
    )
    return jax.shard_map(
        body, mesh=mesh, in_specs=placed, out_specs=P("req", None, "tp"), check_vma=False
    )
```

```python
import functools
import math

import jax
import jax.numpy as jnp
from jax import lax
from jax.experimental import pallas as pl
from jax.experimental.pallas import tpu as pltpu
from jax.sharding import PartitionSpec as P

D = 3200
HEADS = 16
HEAD_DIM = 128
MESH = pl.DeviceIdType.MESH
SIDE = 8
SLAB = 400
BLOCKS = (0, 1, 3, 4, 6, 7, 9, 10, 2, 5, 8, 11)
PART = ((0, 200), (200, 200))
HALF = 104
TOK = 384
SHARE = 800


def shard_of(z, y, core):
    return (z * SIDE + y) * 2 + core


def gather_kernel(
    w_qkv, w_out, gain, tokens, out, permuted_out, share_out,
    mine, held, normed, permuted, token_share,
    own_sem, send_sem, pair_sem, token_sem, write_sem, r1, r2,
):
    me = lax.axis_index("req")
    z = me // (2 * SIDE)
    y = (me // 2) % SIDE
    core = me % 2
    partner = shard_of(z, y, 1 - core)

    def up(v, by):
        return lax.rem(v + by + SIDE, SIDE)

    def ident(part, p, q):
        return shard_of(p, q, core) if part == 0 else shard_of(q, p, core)

    where = ((z, y), (y, z))
    around = [shard_of(up(z, 1), y, core), shard_of(up(z, -1), y, core)]
    across = [shard_of(z, up(y, 1), core), shard_of(z, up(y, -1), core)]
    first = (around, across)
    second = (across, around)

    barrier = pltpu.get_barrier_semaphore()
    for other in around + across + [partner]:
        pl.semaphore_signal(barrier, inc=1, device_id={"req": other}, device_id_type=MESH)
    token_load = pltpu.make_async_copy(tokens, held, token_sem)
    token_load.start()

    last = jnp.zeros((16, 128), jnp.float32)
    row = lax.broadcasted_iota(jnp.int32, (16, 128), 0)
    for b in range(16):
        weight, at = (w_qkv, 128 * BLOCKS[b]) if b < 12 else (w_out, 128 * (b - 12))
        mine[24 * b : 24 * b + 24] = weight[:24, at : at + 128]
        end = weight[24:25, at : at + 128].astype(jnp.float32)
        last = jnp.where(row == b, end, last)
    mine[384:400] = last.astype(jnp.bfloat16)
    pl.semaphore_wait(barrier, 5)

    own = pltpu.make_async_copy(mine, out.at[me], own_sem)
    own.start()

    def piece(part, half):
        low, rows = PART[part]
        if half is None:
            return low, rows
        return (low, HALF) if half == 0 else (low + HALF, rows - HALF)

    def copy(shard, part, half, sem, to, source=None):
        low, rows = piece(part, half)
        dst = out.at[shard, pl.ds(low, rows)]
        src = dst if source is None else source.at[pl.ds(low, rows)]
        return pltpu.make_async_remote_copy(
            src_ref=src,
            dst_ref=dst,
            send_sem=send_sem,
            recv_sem=sem,
            device_id={"req": to},
            device_id_type=MESH,
        )

    def spread(part, j, shard, source=None):
        for way in range(2):
            copy(shard, part, None, r2.at[part, way, 0, j], second[part][way], source).start()
        copy(shard, part, None, pair_sem, partner, source).start()

    for part in range(2):
        for way in range(2):
            copy(me, part, None, r1.at[part, way, 0], first[part][way], mine).start()
    for part in range(2):
        spread(part, 0, me, mine)
    for k in range(1, 5):
        for part in range(2):
            p, q = where[part]
            if k < 4:
                for way in range(2):
                    shard = ident(part, up(p, -k if way == 0 else k), q)
                    copy(shard, part, None, r1.at[part, way, k - 1], partner).wait_recv()
                    half = None if k < 3 else way
                    copy(shard, part, half, r1.at[part, way, k], first[part][way]).start()
                    spread(part, 2 * k - 1 + way, shard)
            else:
                shard = ident(part, up(p, 4), q)
                for way in range(2):
                    copy(shard, part, way, r1.at[part, way, 3], partner).wait_recv()
                spread(part, 7, shard)
    token_load.wait()
    square = jnp.zeros((TOK, 128), jnp.float32)
    for j in range(25):
        x = held[:, 128 * j : 128 * (j + 1)].astype(jnp.float32)
        square += x * x
    scale = lax.rsqrt(jnp.sum(square, axis=1, keepdims=True) / D + 1e-06)
    for j in range(25):
        x = held[:, 128 * j : 128 * (j + 1)].astype(jnp.float32)
        normed[:, 128 * j : 128 * (j + 1)] = (x * scale * gain[j : j + 1]).astype(jnp.bfloat16)

    for h in range(1, 5):

        def step(j, carry):
            sign = 1 - 2 * (j % 2)
            off = ((j + 1) // 2) * sign
            for part in range(2):
                p, q = where[part]
                p_here = up(p, off)
                if h < 4:
                    for way in range(2):
                        shard = ident(part, p_here, up(q, -h if way == 0 else h))
                        copy(shard, part, None, r2.at[part, way, h - 1, j], partner).wait_recv()
                        half = None if h < 3 else way
                        copy(shard, part, half, r2.at[part, way, h, j], second[part][way]).start()
                        copy(shard, part, None, pair_sem, partner).start()
                else:
                    shard = ident(part, p_here, up(q, 4))
                    for way in range(2):
                        copy(shard, part, way, r2.at[part, way, 3, j], partner).wait_recv()
                    copy(shard, part, None, pair_sem, partner).start()
            if h < 4:
                base = 128 * (8 * (h - 1) + j)
                start = jnp.minimum((base + base // 24) // 128 * 128, D - 384)
                start = pl.multiple_of(start, 128)
                source = lax.broadcasted_iota(jnp.int32, (384, 128), 0) + start
                target = lax.broadcasted_iota(jnp.int32, (384, 128), 1) + base
                pick = (source == target + target // 24).astype(jnp.bfloat16)
                permuted[:, pl.ds(pl.multiple_of(base, 128), 128)] = jnp.dot(
                    normed[:, pl.ds(start, 384)], pick, preferred_element_type=jnp.float32
                ).astype(jnp.bfloat16)
            return carry

        lax.fori_loop(0, SIDE, step, 0)
        if h == 2:
            source = lax.broadcasted_iota(jnp.int32, (D, 128), 0)
            target = lax.broadcasted_iota(jnp.int32, (D, 128), 1)
            pick = (source == target * 25 + 24).astype(jnp.bfloat16)
            permuted[:, 3072:] = jnp.dot(
                normed[...], pick, preferred_element_type=jnp.float32
            ).astype(jnp.bfloat16)
        if h == 3:
            tp = lax.axis_index("tp")
            window = held[:, pl.ds(pl.multiple_of(tp * 768, 128), 896)]
            row = lax.broadcasted_iota(jnp.int32, (SHARE, 896), 0)
            lane = lax.broadcasted_iota(jnp.int32, (SHARE, 896), 1)
            feature = jnp.where(row < 768, row + row // 24, (row - 768) * 25 + 24)
            pick = (lane == feature + 32 * tp).astype(jnp.bfloat16)
            token_share[...] = lax.dot_general(
                pick, window, (((1,), (1,)), ((), ())), preferred_element_type=jnp.float32
            ).astype(jnp.bfloat16)
            writes = [
                pltpu.make_async_copy(permuted, permuted_out, write_sem.at[0]),
                pltpu.make_async_copy(token_share, share_out, write_sem.at[1]),
            ]
            for write in writes:
                write.start()

    own.wait()
    for write in writes:
        write.wait()
    half_all = out.at[pl.ds(0, 64)]
    pltpu.make_async_copy(half_all, half_all, pair_sem).wait()
    sent = out.at[pl.ds(0, 127)]
    pltpu.make_async_copy(sent, sent, send_sem).wait()


def gather_weights(w_qkv, w_out, gain, tokens):
    vmem, anywhere = pl.BlockSpec(memory_space=pltpu.VMEM), pl.BlockSpec(memory_space=pl.ANY)
    bf16 = jnp.bfloat16
    return pl.pallas_call(
        gather_kernel,
        out_shape=(
            jax.ShapeDtypeStruct((lax.axis_size("req"), SLAB, 128), bf16),
            jax.ShapeDtypeStruct((TOK, D), bf16),
            jax.ShapeDtypeStruct((SHARE, TOK), bf16),
        ),
        in_specs=[vmem, vmem, vmem, anywhere],
        out_specs=(anywhere, anywhere, anywhere),
        scratch_shapes=[
            pltpu.VMEM((SLAB, 128), bf16),
            pltpu.VMEM((TOK, D), bf16),
            pltpu.VMEM((TOK, D), bf16),
            pltpu.VMEM((TOK, D), bf16),
            pltpu.VMEM((SHARE, TOK), bf16),
            pltpu.SemaphoreType.DMA,
            pltpu.SemaphoreType.DMA,
            pltpu.SemaphoreType.DMA,
            pltpu.SemaphoreType.DMA,
            pltpu.SemaphoreType.DMA((2,)),
            pltpu.SemaphoreType.DMA((2, 2, 4)),
            pltpu.SemaphoreType.DMA((2, 2, 4, SIDE)),
        ],
        compiler_params=pltpu.CompilerParams(
            collective_id=0, has_side_effects=True, vmem_limit_bytes=60 << 20
        ),
        name="gather_weights",
    )(w_qkv, w_out, gain, tokens)


def as_column(row):
    n = row.shape[1]
    return jnp.transpose(jnp.broadcast_to(row, (128, n)))[:, :1]


def finish_kernel(
    x_hbm, share_hbm, q_gain, k_gain, grids, owners, p_gain, p_bias, gathered,
    out,
    x_ref, token_share, wq, wo_raw, last_raw, last_wide, left, slot_owner, wo, proj, v_t, att, own_part, hold, sums, relay_in, final_in, hidden,
    stat_mine, stat_in, row_mine, row_in, picks, members, raws, slots,
    load_sem, stat_sem, row_sem, relay_sem, final_sem, send_sem, out_sem, own_sem,
):
    me = lax.axis_index("req")
    tp = lax.axis_index("tp")
    z = me // (2 * SIDE)
    devices = lax.axis_size("req")
    right = lax.rem(tp + 1, 4)
    opposite = lax.rem(tp + 2, 4)
    left_x = lax.rem(tp + 3, 4)

    def load_block(i):
        at = pl.multiple_of(48 * i, 8)
        return pltpu.make_async_copy(gathered.at[:, pl.ds(at, 48)], wq.at[i], load_sem.at[i])

    wo_load = pltpu.make_async_copy(gathered.at[:, pl.ds(288, 96)], wo_raw, load_sem.at[6])
    last_load = pltpu.make_async_copy(gathered.at[:, pl.ds(384, 16)], last_raw, load_sem.at[7])
    x_load = pltpu.make_async_copy(x_hbm, x_ref, load_sem.at[8])
    share_load = pltpu.make_async_copy(share_hbm, token_share, load_sem.at[9])
    for load in (last_load, x_load, load_block(0), load_block(1)):
        load.start()

    barrier = pltpu.get_barrier_semaphore()

    def greet(i, carry):
        other = lax.rem(me + i, devices)
        pl.semaphore_signal(barrier, inc=1, device_id={"req": other}, device_id_type=MESH)
        return carry

    lax.fori_loop(1, devices, greet, 0)
    for other in (right, opposite, left_x):
        pl.semaphore_signal(barrier, inc=1, device_id={"tp": other}, device_id_type=MESH)

    last_load.wait()
    last_wide[...] = last_raw[...].astype(jnp.float32)
    for b in range(16):
        left[:, 128 * b : 128 * (b + 1)] = last_wide[:, b, :].astype(jnp.bfloat16)

    def project(i, carry):
        load_block(i).wait()

        @pl.when(i < 4)
        def _():
            load_block(i + 2).start()

        weight = jnp.concatenate(
            [wq[i, :, :24].reshape(3072, 128), wq[i, :, 24:].reshape(3072, 128)], axis=1
        )
        at = pl.multiple_of(i * 256, 256)
        total = jnp.dot(x_ref[:, :3072], weight, preferred_element_type=jnp.float32)
        total += jnp.dot(
            x_ref[:, 3072:], left[:, pl.ds(at, 256)], preferred_element_type=jnp.float32
        )
        proj[:, pl.ds(at, 256)] = total
        return carry

    x_load.wait()
    lax.fori_loop(0, 4, project, 0)
    wo_load.start()
    share_load.start()

    pl.semaphore_wait(barrier, devices - 1 + 3)

    def to_row(other, mine, into, sem, total_sem):
        return pltpu.make_async_remote_copy(
            src_ref=mine,
            dst_ref=into.at[tp],
            send_sem=total_sem,
            recv_sem=sem,
            device_id={"tp": other},
            device_id_type=MESH,
        )

    q_sum = jnp.zeros((TOK, 1), jnp.float32)
    k_sum = jnp.zeros((TOK, 1), jnp.float32)
    for h in range(4):
        q = proj[:, h * 256 : h * 256 + 128]
        k = proj[:, h * 256 + 128 : h * 256 + 256]
        q_sum += jnp.sum(q * q, axis=1, keepdims=True)
        k_sum += jnp.sum(k * k, axis=1, keepdims=True)
    lane = lax.broadcasted_iota(jnp.int32, (TOK, 128), 1)
    both = jnp.where(lane == 0, q_sum, jnp.where(lane == 1, k_sum, 0.0))
    stat_mine[...] = jnp.transpose(both)[:8]
    stat_in[pl.ds(tp, 1)] = stat_mine[...][None]
    stat_copies = [
        to_row(o, stat_mine, stat_in, stat_sem.at[0], stat_sem.at[1])
        for o in (opposite, right, left_x)
    ]
    for c in stat_copies:
        c.start()

    lax.fori_loop(4, 6, project, 0)
    for h in range(4):
        v_t[h] = jnp.transpose(proj[:, 1024 + h * 128 : 1152 + h * 128]).astype(jnp.bfloat16)
    wo_load.wait()

    def pack(t, carry):
        at = pl.multiple_of(t * 32, 32)
        for b in range(4):
            block = wo_raw[pl.ds(at, 32), b * 24 : (b + 1) * 24]
            wo[t, :768, b * 128 : (b + 1) * 128] = block.reshape(768, 128)
        wo[t, 768:] = left[pl.ds(at, 32), 1536:]
        return carry

    lax.fori_loop(0, 4, pack, 0)

    ends = []
    total = 0
    for i in range(3):
        total = total + grids[0, i] * grids[1, i]
        ends.append(total)

    def segment(ids, scale):
        found = jnp.zeros(ids.shape, jnp.int32)
        for e in ends:
            found += (ids >= scale * e).astype(jnp.int32)
        return found

    key_segment = segment(lax.broadcasted_iota(jnp.int32, (TOK, 128), 0), 4)

    pltpu.make_async_copy(stat_in.at[pl.ds(0, 3)], stat_in.at[pl.ds(0, 3)], stat_sem.at[0]).wait()
    totals = stat_in[0] + stat_in[1] + stat_in[2] + stat_in[3]
    scales = lax.rsqrt(totals / (HEADS * HEAD_DIM) + 1e-06)
    q_scale = as_column(scales[0:1])
    k_scale = as_column(scales[1:2])
    for h in range(4):
        at = h * 256
        head = slice(h * 128, (h + 1) * 128)
        proj[:, at : at + 128] = proj[:, at : at + 128] * q_scale * q_gain[:, head]
        proj[:, at + 128 : at + 256] = proj[:, at + 128 : at + 256] * k_scale * k_gain[:, head]

    def push(source, into, sem, other):
        return pltpu.make_async_remote_copy(
            src_ref=source,
            dst_ref=into,
            send_sem=send_sem.at[0],
            recv_sem=sem,
            device_id={"tp": other},
            device_id_type=MESH,
        )

    low, high = pl.ds(0, 400), pl.ds(400, 400)

    def relay(b):
        for way, (rows, other) in enumerate(((low, right), (high, left_x))):
            push(relay_in.at[way, b], relay_in.at[way, b], relay_sem.at[way, b], other).wait_recv()
            total = hold[way, b] + relay_in[way, b].astype(jnp.float32)
            sums[1 + way, b, rows] = total.astype(jnp.bfloat16)
            push(
                sums.at[1 + way, b, rows], final_in.at[way, b, rows],
                final_sem.at[way, b, 1], other,
            ).start()

    for b in range(3):
        q_at = slice(b * 128, (b + 1) * 128)
        same = key_segment == segment(
            lax.broadcasted_iota(jnp.int32, (TOK, 128), 1) + 128 * b, 4
        )
        for h in range(4):
            at = h * 256
            scores = lax.dot_general(
                proj[:, at + 128 : at + 256],
                proj[q_at, at : at + 128],
                (((1,), (1,)), ((), ())),
                precision=lax.Precision.HIGHEST,
                preferred_element_type=jnp.float32,
            ) * (1.0 / math.sqrt(HEAD_DIM))
            scores = jnp.where(same, scores, -1e30)
            raw = jnp.exp(scores - jnp.max(scores, axis=0, keepdims=True))
            probs = (raw * (1.0 / jnp.sum(raw, axis=0, keepdims=True))).astype(jnp.bfloat16)
            att[b, h * 128 : (h + 1) * 128] = jnp.dot(
                v_t[h], probs, preferred_element_type=jnp.float32
            ).astype(jnp.bfloat16)
        attended = att[b]

        def term(t):
            return jnp.dot(wo[t], attended, preferred_element_type=jnp.float32)

        sums[0, b] = term(opposite).astype(jnp.bfloat16)
        push(sums.at[0, b, low], relay_in.at[0, b], relay_sem.at[0, b], right).start()
        push(sums.at[0, b, high], relay_in.at[1, b], relay_sem.at[1, b], left_x).start()
        to_right = term(right)
        sums[1, b, high] = to_right[400:].astype(jnp.bfloat16)
        push(
            sums.at[1, b, high], final_in.at[0, b, high], final_sem.at[0, b, 0], right
        ).start()
        hold[0, b] = to_right[:400]
        to_left = term(left_x)
        sums[2, b, low] = to_left[:400].astype(jnp.bfloat16)
        push(
            sums.at[2, b, low], final_in.at[1, b, low], final_sem.at[1, b, 0], left_x
        ).start()
        hold[1, b] = to_left[400:]
        own_part[b] = term(tp)
        if b > 0:
            relay(b - 1)
    relay(2)

    slot = lax.broadcasted_iota(jnp.int32, (1, 128), 1)
    image = segment(slot, 1)
    slot_owner[...] = jnp.full((1, 128), -1, jnp.int32)
    slot_owner[:, : owners.shape[1]] = owners[...]
    owner = jnp.where(image < 3, slot_owner[...], -1)
    cols = jnp.ones((1, 128), jnp.int32)
    start = jnp.zeros((1, 128), jnp.int32)
    for i in range(3):
        cols = jnp.where(image == i, grids[1, i], cols)
        if i:
            start = jnp.where(image == i, ends[i - 1], start)
    offset = slot - start
    row_half = jnp.zeros((1, 128), jnp.int32)
    for i in range(1, 48):
        row_half += (offset >= i * cols).astype(jnp.int32)
    first_row = 2 * start + offset + row_half * cols
    first_row = 2 * first_row
    owner_square = jnp.broadcast_to(owner, (128, 128))
    owner_down = jnp.transpose(owner_square)
    earlier = lax.broadcasted_iota(jnp.int32, (128, 128), 0) < lax.broadcasted_iota(
        jnp.int32, (128, 128), 1
    )
    rank = jnp.sum(
        jnp.where((owner_down == owner_square) & earlier, 1, 0), axis=0, keepdims=True
    )

    def table(i, carry):
        base = 16 * i
        line = lax.broadcasted_iota(jnp.int32, (128, 128), 0)
        found = (owner == base + line // 8) & (rank == (line // 4) % 2)
        first = jnp.sum(jnp.where(found, first_row, 0), axis=1, keepdims=True)
        across = 2 * jnp.sum(jnp.where(found, cols, 0), axis=1, keepdims=True)
        filled = across > 0
        first = jnp.where(filled, first, -10000)
        part = lax.broadcasted_iota(jnp.int32, (128, 1), 0) % 4
        token = lax.broadcasted_iota(jnp.int32, (128, TOK), 1)
        mine = first + part % 2 + (part // 2) * across
        picks[i] = (token == mine).astype(jnp.bfloat16)
        upper, lower = token - first, token - first - across
        any_part = (upper == 0) | (upper == 1) | (lower == 0) | (lower == 1)
        members[i] = any_part.astype(jnp.float32)
        return carry

    lax.fori_loop(0, SIDE, table, 0)

    share_load.wait()
    row = lax.broadcasted_iota(jnp.int32, (SHARE, SHARE), 0)
    column = lax.broadcasted_iota(jnp.int32, (SHARE, SHARE), 1)
    feature = jnp.where(column < 768, column + column // 24, (column - 768) * 25 + 24)
    unpick = (row == feature).astype(jnp.bfloat16)
    for b in range(3):
        for way, rows in ((0, (low, high)), (1, (high, low))):
            for i in range(2):
                here = final_in.at[way, b, rows[i]]
                push(here, here, final_sem.at[way, b, 1 - i], right).wait_recv()
        total = own_part[b] + final_in[0, b].astype(jnp.float32)
        total += final_in[1, b].astype(jnp.float32)
        total += token_share[:, b * 128 : (b + 1) * 128].astype(jnp.float32)
        rounded = jnp.dot(unpick, total.astype(jnp.bfloat16), preferred_element_type=jnp.float32)
        hidden[:, b * 128 : (b + 1) * 128] = rounded.astype(jnp.bfloat16)
        row_mine[0:1, b * 128 : (b + 1) * 128] = jnp.sum(rounded, axis=0, keepdims=True)
        row_mine[1:2, b * 128 : (b + 1) * 128] = jnp.sum(rounded * rounded, axis=0, keepdims=True)
    row_mine[2:] = jnp.zeros((6, TOK), jnp.float32)
    row_in[pl.ds(tp, 1)] = row_mine[...][None]
    row_copies = [
        to_row(o, row_mine, row_in, row_sem.at[0], row_sem.at[1])
        for o in (opposite, right, left_x)
    ]
    for c in row_copies:
        c.start()

    def gather_rows(i, carry):
        raws[i] = lax.dot_general(
            picks[i], hidden[...], (((1,), (1,)), ((), ())), preferred_element_type=jnp.float32
        )
        return carry

    lax.fori_loop(0, SIDE, gather_rows, 0)

    pltpu.make_async_copy(row_in.at[pl.ds(0, 3)], row_in.at[pl.ds(0, 3)], row_sem.at[0]).wait()
    row_total = row_in[0] + row_in[1] + row_in[2] + row_in[3]
    sum_row = row_total[0:1]
    square_row = row_total[1:2]
    gain = jnp.concatenate([p_gain[...], p_gain[...]], axis=0)[None]
    bias = jnp.concatenate([p_bias[...], p_bias[...]], axis=0)[None]

    def alternate(i):
        return ((i + 1) // 2) * (1 - 2 * ((i + 1) % 2))

    def fill_plane(i, carry):
        member = members[i]
        mean = jnp.sum(member * sum_row, axis=1, keepdims=True) / (4 * D)
        square = jnp.sum(member * square_row, axis=1, keepdims=True) / (4 * D)
        filled = jnp.sum(member, axis=1, keepdims=True) > 0.5
        scale = lax.rsqrt(square - mean * mean + 1e-05)
        value = ((raws[i] - mean) * scale).reshape(16, 8, SHARE) * gain + bias
        value = jnp.where(filled, value.reshape(128, SHARE), 0.0)
        slots[pl.ds(16 * i, 16)] = value.reshape(16, 2, 4, SHARE).astype(jnp.bfloat16)
        return carry

    y = (me // 2) % SIDE
    core = me % 2

    def send(i, carry):
        to_z = lax.rem(z + alternate((15 - i % 8 - i // 8) % 8) + SIDE, SIDE)
        to_y = lax.rem(y + alternate(7 - i % 8) + SIDE, SIDE)
        for flip in range(2):
            other = shard_of(to_z, to_y, lax.rem(core + flip, 2))

            @pl.when(other != me)
            def _():
                pltpu.make_async_remote_copy(
                    src_ref=slots.at[other],
                    dst_ref=out.at[me],
                    send_sem=send_sem.at[1],
                    recv_sem=out_sem,
                    device_id={"req": other},
                    device_id_type=MESH,
                ).start()

        return carry

    lax.fori_loop(0, SIDE, fill_plane, 0)
    lax.fori_loop(0, SIDE * SIDE, send, 0)
    keep = pltpu.make_async_copy(slots.at[me], out.at[me], own_sem)
    keep.start()
    keep.wait()
    pltpu.make_async_copy(stat_in.at[pl.ds(0, 3)], stat_in.at[pl.ds(0, 3)], stat_sem.at[1]).wait()
    pltpu.make_async_copy(row_in.at[pl.ds(0, 3)], row_in.at[pl.ds(0, 3)], row_sem.at[1]).wait()
    pltpu.make_async_copy(sums, sums, send_sem.at[0]).wait()
    most = out.at[pl.ds(0, 127)]
    pltpu.make_async_copy(most, most, send_sem.at[1]).wait()
    pltpu.make_async_copy(most, most, out_sem).wait()


def finish(x, token_share, q_gain, k_gain, grids, owners, p_gain, p_bias, gathered):
    vmem = pl.BlockSpec(memory_space=pltpu.VMEM)
    bf16, f32 = jnp.bfloat16, jnp.float32
    dma = pltpu.SemaphoreType.DMA
    return pl.pallas_call(
        finish_kernel,
        out_shape=jax.ShapeDtypeStruct((128, 2, 4, SHARE), bf16),
        in_specs=[pl.BlockSpec(memory_space=pl.ANY)] * 2
        + [vmem] * 2
        + [pl.BlockSpec(memory_space=pltpu.SMEM)]
        + [vmem] * 3
        + [pl.BlockSpec(memory_space=pl.ANY)],
        out_specs=pl.BlockSpec(memory_space=pl.ANY),
        scratch_shapes=[
            pltpu.VMEM((TOK, D), bf16),
            pltpu.VMEM((SHARE, TOK), bf16),
            pltpu.VMEM((6, 128, 48, 128), bf16),
            pltpu.VMEM((128, 96, 128), bf16),
            pltpu.VMEM((128, 16, 128), bf16),
            pltpu.VMEM((128, 16, 128), f32),
            pltpu.VMEM((128, 2048), bf16),
            pltpu.VMEM((1, 128), jnp.int32),
            pltpu.VMEM((4, SHARE, 512), bf16),
            pltpu.VMEM((TOK, 1536), f32),
            pltpu.VMEM((4, 128, TOK), bf16),
            pltpu.VMEM((3, 512, 128), bf16),
            pltpu.VMEM((3, SHARE, 128), f32),
            pltpu.VMEM((2, 3, 400, 128), f32),
            pltpu.VMEM((3, 3, SHARE, 128), bf16),
            pltpu.VMEM((2, 3, 400, 128), bf16),
            pltpu.VMEM((2, 3, SHARE, 128), bf16),
            pltpu.VMEM((SHARE, TOK), bf16),
            pltpu.VMEM((8, TOK), f32),
            pltpu.VMEM((4, 8, TOK), f32),
            pltpu.VMEM((8, TOK), f32),
            pltpu.VMEM((4, 8, TOK), f32),
            pltpu.VMEM((SIDE, 128, TOK), bf16),
            pltpu.VMEM((SIDE, 128, TOK), f32),
            pltpu.VMEM((SIDE, 128, SHARE), f32),
            pltpu.VMEM((128, 2, 4, SHARE), bf16),
            dma((10,)),
            dma((2,)),
            dma((2,)),
            dma((2, 3)),
            dma((2, 3, 2)),
            dma((2,)),
            dma,
            dma,
        ],
        compiler_params=pltpu.CompilerParams(
            collective_id=1, has_side_effects=True, vmem_limit_bytes=60 << 20
        ),
        name="finish",
    )(x, token_share, q_gain, k_gain, grids, owners, p_gain, p_bias, gathered)


def body(tokens, norm_gain, w_qkv, q_gain, k_gain, w_out, grids, owners, proj_gain, proj_bias):
    gathered, normed, token_share = gather_weights(
        w_qkv, w_out.T, norm_gain.reshape(-1, 128), tokens
    )
    arrived = finish(
        normed, token_share, q_gain.reshape(1, -1), k_gain.reshape(1, -1),
        grids.T, owners.reshape(1, -1), proj_gain, proj_bias, gathered,
    )
    return arrived.reshape(-1, 4, SHARE)


def solution(mesh):
    placed = (
        P("req", None),
        P(),
        P("req", "tp"),
        P("tp"),
        P("tp"),
        P("tp", "req"),
        P("req", None),
        P("req"),
        P(None, "tp"),
        P(None, "tp"),
    )
    return jax.shard_map(
        body, mesh=mesh, in_specs=placed, out_specs=P("req", None, "tp"), check_vma=False
    )
```

```python
import functools
import math

import jax
import jax.numpy as jnp
from jax import lax
from jax.experimental import pallas as pl
from jax.experimental.pallas import tpu as pltpu
from jax.sharding import PartitionSpec as P

D = 3200
HEADS = 16
HEAD_DIM = 128
MESH = pl.DeviceIdType.MESH
SIDE = 8
SLAB = 400
BLOCKS = (0, 1, 3, 4, 6, 7, 9, 10, 2, 5, 8, 11)
PART = ((0, 200), (200, 200))
HALF = 104
TOK = 384
SHARE = 800


def shard_of(z, y, core):
    return (z * SIDE + y) * 2 + core


def gather_kernel(
    w_qkv, w_out, gain, tokens, out, permuted_out, share_out,
    mine, held, normed, permuted, token_share,
    own_sem, send_sem, pair_sem, token_sem, write_sem, r1, r2,
):
    me = lax.axis_index("req")
    z = me // (2 * SIDE)
    y = (me // 2) % SIDE
    core = me % 2
    partner = shard_of(z, y, 1 - core)

    def up(v, by):
        return lax.rem(v + by + SIDE, SIDE)

    def ident(part, p, q):
        return shard_of(p, q, core) if part == 0 else shard_of(q, p, core)

    where = ((z, y), (y, z))
    around = [shard_of(up(z, 1), y, core), shard_of(up(z, -1), y, core)]
    across = [shard_of(z, up(y, 1), core), shard_of(z, up(y, -1), core)]
    first = (around, across)
    second = (across, around)

    barrier = pltpu.get_barrier_semaphore()
    for other in around + across + [partner]:
        pl.semaphore_signal(barrier, inc=1, device_id={"req": other}, device_id_type=MESH)
    token_load = pltpu.make_async_copy(tokens, held, token_sem)
    token_load.start()

    last = jnp.zeros((16, 128), jnp.float32)
    row = lax.broadcasted_iota(jnp.int32, (16, 128), 0)
    for b in range(16):
        weight, at = (w_qkv, 128 * BLOCKS[b]) if b < 12 else (w_out, 128 * (b - 12))
        mine[24 * b : 24 * b + 24] = weight[:24, at : at + 128]
        end = weight[24:25, at : at + 128].astype(jnp.float32)
        last = jnp.where(row == b, end, last)
    mine[384:400] = last.astype(jnp.bfloat16)
    pl.semaphore_wait(barrier, 5)

    own = pltpu.make_async_copy(mine, out.at[me], own_sem)
    own.start()

    def piece(part, half):
        low, rows = PART[part]
        if half is None:
            return low, rows
        return (low, HALF) if half == 0 else (low + HALF, rows - HALF)

    def copy(shard, part, half, sem, to, source=None):
        low, rows = piece(part, half)
        dst = out.at[shard, pl.ds(low, rows)]
        src = dst if source is None else source.at[pl.ds(low, rows)]
        return pltpu.make_async_remote_copy(
            src_ref=src,
            dst_ref=dst,
            send_sem=send_sem,
            recv_sem=sem,
            device_id={"req": to},
            device_id_type=MESH,
        )

    def spread(part, j, shard, source=None):
        for way in range(2):
            copy(shard, part, None, r2.at[part, way, 0, j], second[part][way], source).start()
        copy(shard, part, None, pair_sem, partner, source).start()

    for part in range(2):
        for way in range(2):
            copy(me, part, None, r1.at[part, way, 0], first[part][way], mine).start()
    for part in range(2):
        spread(part, 0, me, mine)
    for k in range(1, 5):
        for part in range(2):
            p, q = where[part]
            if k < 4:
                for way in range(2):
                    shard = ident(part, up(p, -k if way == 0 else k), q)
                    copy(shard, part, None, r1.at[part, way, k - 1], partner).wait_recv()
                    half = None if k < 3 else way
                    copy(shard, part, half, r1.at[part, way, k], first[part][way]).start()
                    spread(part, 2 * k - 1 + way, shard)
            else:
                shard = ident(part, up(p, 4), q)
                for way in range(2):
                    copy(shard, part, way, r1.at[part, way, 3], partner).wait_recv()
                spread(part, 7, shard)
    token_load.wait()
    square = jnp.zeros((TOK, 128), jnp.float32)
    for j in range(25):
        x = held[:, 128 * j : 128 * (j + 1)].astype(jnp.float32)
        square += x * x
    scale = lax.rsqrt(jnp.sum(square, axis=1, keepdims=True) / D + 1e-06)
    for j in range(25):
        x = held[:, 128 * j : 128 * (j + 1)].astype(jnp.float32)
        normed[:, 128 * j : 128 * (j + 1)] = (x * scale * gain[j : j + 1]).astype(jnp.bfloat16)

    for h in range(1, 5):

        def step(j, carry):
            sign = 1 - 2 * (j % 2)
            off = ((j + 1) // 2) * sign
            for part in range(2):
                p, q = where[part]
                p_here = up(p, off)
                if h < 4:
                    for way in range(2):
                        shard = ident(part, p_here, up(q, -h if way == 0 else h))
                        copy(shard, part, None, r2.at[part, way, h - 1, j], partner).wait_recv()
                        half = None if h < 3 else way
                        copy(shard, part, half, r2.at[part, way, h, j], second[part][way]).start()
                        copy(shard, part, None, pair_sem, partner).start()
                else:
                    shard = ident(part, p_here, up(q, 4))
                    for way in range(2):
                        copy(shard, part, way, r2.at[part, way, 3, j], partner).wait_recv()
                    copy(shard, part, None, pair_sem, partner).start()
            if h < 4:
                base = 128 * (8 * (h - 1) + j)
                start = jnp.minimum((base + base // 24) // 128 * 128, D - 384)
                start = pl.multiple_of(start, 128)
                source = lax.broadcasted_iota(jnp.int32, (384, 128), 0) + start
                target = lax.broadcasted_iota(jnp.int32, (384, 128), 1) + base
                pick = (source == target + target // 24).astype(jnp.bfloat16)
                permuted[:, pl.ds(pl.multiple_of(base, 128), 128)] = jnp.dot(
                    normed[:, pl.ds(start, 384)], pick, preferred_element_type=jnp.float32
                ).astype(jnp.bfloat16)
            return carry

        lax.fori_loop(0, SIDE, step, 0)
        if h == 2:
            source = lax.broadcasted_iota(jnp.int32, (D, 128), 0)
            target = lax.broadcasted_iota(jnp.int32, (D, 128), 1)
            pick = (source == target * 25 + 24).astype(jnp.bfloat16)
            permuted[:, 3072:] = jnp.dot(
                normed[...], pick, preferred_element_type=jnp.float32
            ).astype(jnp.bfloat16)
        if h == 3:
            tp = lax.axis_index("tp")
            window = held[:, pl.ds(pl.multiple_of(tp * 768, 128), 896)]
            row = lax.broadcasted_iota(jnp.int32, (SHARE, 896), 0)
            lane = lax.broadcasted_iota(jnp.int32, (SHARE, 896), 1)
            feature = jnp.where(row < 768, row + row // 24, (row - 768) * 25 + 24)
            pick = (lane == feature + 32 * tp).astype(jnp.bfloat16)
            token_share[...] = lax.dot_general(
                pick, window, (((1,), (1,)), ((), ())), preferred_element_type=jnp.float32
            ).astype(jnp.bfloat16)
            writes = [
                pltpu.make_async_copy(permuted, permuted_out, write_sem.at[0]),
                pltpu.make_async_copy(token_share, share_out, write_sem.at[1]),
            ]
            for write in writes:
                write.start()

    own.wait()
    for write in writes:
        write.wait()
    half_all = out.at[pl.ds(0, 64)]
    pltpu.make_async_copy(half_all, half_all, pair_sem).wait()
    sent = out.at[pl.ds(0, 127)]
    pltpu.make_async_copy(sent, sent, send_sem).wait()


def gather_weights(w_qkv, w_out, gain, tokens):
    vmem, anywhere = pl.BlockSpec(memory_space=pltpu.VMEM), pl.BlockSpec(memory_space=pl.ANY)
    bf16 = jnp.bfloat16
    return pl.pallas_call(
        gather_kernel,
        out_shape=(
            jax.ShapeDtypeStruct((lax.axis_size("req"), SLAB, 128), bf16),
            jax.ShapeDtypeStruct((TOK, D), bf16),
            jax.ShapeDtypeStruct((SHARE, TOK), bf16),
        ),
        in_specs=[vmem, vmem, vmem, anywhere],
        out_specs=(anywhere, anywhere, anywhere),
        scratch_shapes=[
            pltpu.VMEM((SLAB, 128), bf16),
            pltpu.VMEM((TOK, D), bf16),
            pltpu.VMEM((TOK, D), bf16),
            pltpu.VMEM((TOK, D), bf16),
            pltpu.VMEM((SHARE, TOK), bf16),
            pltpu.SemaphoreType.DMA,
            pltpu.SemaphoreType.DMA,
            pltpu.SemaphoreType.DMA,
            pltpu.SemaphoreType.DMA,
            pltpu.SemaphoreType.DMA((2,)),
            pltpu.SemaphoreType.DMA((2, 2, 4)),
            pltpu.SemaphoreType.DMA((2, 2, 4, SIDE)),
        ],
        compiler_params=pltpu.CompilerParams(
            collective_id=0, has_side_effects=True, vmem_limit_bytes=60 << 20
        ),
        name="gather_weights",
    )(w_qkv, w_out, gain, tokens)


def as_column(row):
    n = row.shape[1]
    return jnp.transpose(jnp.broadcast_to(row, (128, n)))[:, :1]


def finish_kernel(
    x_hbm, share_hbm, q_gain, k_gain, grids, owners, p_gain, p_bias, gathered,
    out, out_end,
    x_ref, token_share, wq, wo_raw, last_raw, last_wide, left, slot_owner, wo, proj, v_t, att, own_part, hold, sums, relay_in, final_in, hidden,
    stat_mine, stat_in, row_mine, row_in, picks, members, raws, slots, slots_end,
    load_sem, stat_sem, row_sem, relay_sem, final_sem, send_sem, out_sem, own_sem,
):
    me = lax.axis_index("req")
    tp = lax.axis_index("tp")
    z = me // (2 * SIDE)
    devices = lax.axis_size("req")
    right = lax.rem(tp + 1, 4)
    opposite = lax.rem(tp + 2, 4)
    left_x = lax.rem(tp + 3, 4)

    def load_block(i):
        at = pl.multiple_of(48 * i, 8)
        return pltpu.make_async_copy(gathered.at[:, pl.ds(at, 48)], wq.at[i], load_sem.at[i])

    wo_load = pltpu.make_async_copy(gathered.at[:, pl.ds(288, 96)], wo_raw, load_sem.at[6])
    last_load = pltpu.make_async_copy(gathered.at[:, pl.ds(384, 16)], last_raw, load_sem.at[7])
    x_load = pltpu.make_async_copy(x_hbm, x_ref, load_sem.at[8])
    share_load = pltpu.make_async_copy(share_hbm, token_share, load_sem.at[9])
    for load in (last_load, x_load, load_block(0), load_block(1)):
        load.start()

    barrier = pltpu.get_barrier_semaphore()

    def greet(i, carry):
        other = lax.rem(me + i, devices)
        pl.semaphore_signal(barrier, inc=1, device_id={"req": other}, device_id_type=MESH)
        return carry

    lax.fori_loop(1, devices, greet, 0)
    for other in (right, opposite, left_x):
        pl.semaphore_signal(barrier, inc=1, device_id={"tp": other}, device_id_type=MESH)

    last_load.wait()
    last_wide[...] = last_raw[...].astype(jnp.float32)
    for b in range(16):
        left[:, 128 * b : 128 * (b + 1)] = last_wide[:, b, :].astype(jnp.bfloat16)

    def project(i, carry):
        load_block(i).wait()

        @pl.when(i < 4)
        def _():
            load_block(i + 2).start()

        weight = jnp.concatenate(
            [wq[i, :, :24].reshape(3072, 128), wq[i, :, 24:].reshape(3072, 128)], axis=1
        )
        at = pl.multiple_of(i * 256, 256)
        total = jnp.dot(x_ref[:, :3072], weight, preferred_element_type=jnp.float32)
        total += jnp.dot(
            x_ref[:, 3072:], left[:, pl.ds(at, 256)], preferred_element_type=jnp.float32
        )
        proj[:, pl.ds(at, 256)] = total
        return carry

    x_load.wait()
    lax.fori_loop(0, 4, project, 0)
    wo_load.start()
    share_load.start()

    pl.semaphore_wait(barrier, devices - 1 + 3)

    def to_row(other, mine, into, sem, total_sem):
        return pltpu.make_async_remote_copy(
            src_ref=mine,
            dst_ref=into.at[tp],
            send_sem=total_sem,
            recv_sem=sem,
            device_id={"tp": other},
            device_id_type=MESH,
        )

    q_sum = jnp.zeros((TOK, 1), jnp.float32)
    k_sum = jnp.zeros((TOK, 1), jnp.float32)
    for h in range(4):
        q = proj[:, h * 256 : h * 256 + 128]
        k = proj[:, h * 256 + 128 : h * 256 + 256]
        q_sum += jnp.sum(q * q, axis=1, keepdims=True)
        k_sum += jnp.sum(k * k, axis=1, keepdims=True)
    lane = lax.broadcasted_iota(jnp.int32, (TOK, 128), 1)
    both = jnp.where(lane == 0, q_sum, jnp.where(lane == 1, k_sum, 0.0))
    stat_mine[...] = jnp.transpose(both)[:8]
    stat_in[pl.ds(tp, 1)] = stat_mine[...][None]
    stat_copies = [
        to_row(o, stat_mine, stat_in, stat_sem.at[0], stat_sem.at[1])
        for o in (opposite, right, left_x)
    ]
    for c in stat_copies:
        c.start()

    lax.fori_loop(4, 6, project, 0)
    for h in range(4):
        v_t[h] = jnp.transpose(proj[:, 1024 + h * 128 : 1152 + h * 128]).astype(jnp.bfloat16)
    wo_load.wait()

    def pack(t, carry):
        at = pl.multiple_of(t * 32, 32)
        for b in range(4):
            block = wo_raw[pl.ds(at, 32), b * 24 : (b + 1) * 24]
            wo[t, :768, b * 128 : (b + 1) * 128] = block.reshape(768, 128)
        wo[t, 768:] = left[pl.ds(at, 32), 1536:]
        return carry

    lax.fori_loop(0, 4, pack, 0)

    ends = []
    total = 0
    for i in range(3):
        total = total + grids[0, i] * grids[1, i]
        ends.append(total)

    def segment(ids, scale):
        found = jnp.zeros(ids.shape, jnp.int32)
        for e in ends:
            found += (ids >= scale * e).astype(jnp.int32)
        return found

    key_segment = segment(lax.broadcasted_iota(jnp.int32, (TOK, 128), 0), 4)

    pltpu.make_async_copy(stat_in.at[pl.ds(0, 3)], stat_in.at[pl.ds(0, 3)], stat_sem.at[0]).wait()
    totals = stat_in[0] + stat_in[1] + stat_in[2] + stat_in[3]
    scales = lax.rsqrt(totals / (HEADS * HEAD_DIM) + 1e-06)
    q_scale = as_column(scales[0:1])
    k_scale = as_column(scales[1:2])
    for h in range(4):
        at = h * 256
        head = slice(h * 128, (h + 1) * 128)
        proj[:, at : at + 128] = proj[:, at : at + 128] * q_scale * q_gain[:, head]
        proj[:, at + 128 : at + 256] = proj[:, at + 128 : at + 256] * k_scale * k_gain[:, head]

    def push(source, into, sem, other):
        return pltpu.make_async_remote_copy(
            src_ref=source,
            dst_ref=into,
            send_sem=send_sem.at[0],
            recv_sem=sem,
            device_id={"tp": other},
            device_id_type=MESH,
        )

    low, high = pl.ds(0, 400), pl.ds(400, 400)

    def relay(b):
        for way, (rows, other) in enumerate(((low, right), (high, left_x))):
            push(relay_in.at[way, b], relay_in.at[way, b], relay_sem.at[way, b], other).wait_recv()
            total = hold[way, b] + relay_in[way, b].astype(jnp.float32)
            sums[1 + way, b, rows] = total.astype(jnp.bfloat16)
            push(
                sums.at[1 + way, b, rows], final_in.at[way, b, rows],
                final_sem.at[way, b, 1], other,
            ).start()

    for b in range(3):
        q_at = slice(b * 128, (b + 1) * 128)
        same = key_segment == segment(
            lax.broadcasted_iota(jnp.int32, (TOK, 128), 1) + 128 * b, 4
        )
        for h in range(4):
            at = h * 256
            scores = lax.dot_general(
                proj[:, at + 128 : at + 256],
                proj[q_at, at : at + 128],
                (((1,), (1,)), ((), ())),
                precision=lax.Precision.HIGHEST,
                preferred_element_type=jnp.float32,
            ) * (1.0 / math.sqrt(HEAD_DIM))
            scores = jnp.where(same, scores, -1e30)
            raw = jnp.exp(scores - jnp.max(scores, axis=0, keepdims=True))
            probs = (raw * (1.0 / jnp.sum(raw, axis=0, keepdims=True))).astype(jnp.bfloat16)
            att[b, h * 128 : (h + 1) * 128] = jnp.dot(
                v_t[h], probs, preferred_element_type=jnp.float32
            ).astype(jnp.bfloat16)
        attended = att[b]

        def term(t):
            return jnp.dot(wo[t], attended, preferred_element_type=jnp.float32)

        sums[0, b] = term(opposite).astype(jnp.bfloat16)
        push(sums.at[0, b, low], relay_in.at[0, b], relay_sem.at[0, b], right).start()
        push(sums.at[0, b, high], relay_in.at[1, b], relay_sem.at[1, b], left_x).start()
        to_right = term(right)
        sums[1, b, high] = to_right[400:].astype(jnp.bfloat16)
        push(
            sums.at[1, b, high], final_in.at[0, b, high], final_sem.at[0, b, 0], right
        ).start()
        hold[0, b] = to_right[:400]
        to_left = term(left_x)
        sums[2, b, low] = to_left[:400].astype(jnp.bfloat16)
        push(
            sums.at[2, b, low], final_in.at[1, b, low], final_sem.at[1, b, 0], left_x
        ).start()
        hold[1, b] = to_left[400:]
        own_part[b] = term(tp)
        if b > 0:
            relay(b - 1)
    relay(2)

    slot = lax.broadcasted_iota(jnp.int32, (1, 128), 1)
    image = segment(slot, 1)
    slot_owner[...] = jnp.full((1, 128), -1, jnp.int32)
    slot_owner[:, : owners.shape[1]] = owners[...]
    owner = jnp.where(image < 3, slot_owner[...], -1)
    cols = jnp.ones((1, 128), jnp.int32)
    start = jnp.zeros((1, 128), jnp.int32)
    for i in range(3):
        cols = jnp.where(image == i, grids[1, i], cols)
        if i:
            start = jnp.where(image == i, ends[i - 1], start)
    offset = slot - start
    row_half = jnp.zeros((1, 128), jnp.int32)
    for i in range(1, 48):
        row_half += (offset >= i * cols).astype(jnp.int32)
    first_row = 2 * start + offset + row_half * cols
    first_row = 2 * first_row
    owner_square = jnp.broadcast_to(owner, (128, 128))
    owner_down = jnp.transpose(owner_square)
    earlier = lax.broadcasted_iota(jnp.int32, (128, 128), 0) < lax.broadcasted_iota(
        jnp.int32, (128, 128), 1
    )
    rank = jnp.sum(
        jnp.where((owner_down == owner_square) & earlier, 1, 0), axis=0, keepdims=True
    )

    def table(i, carry):
        base = 16 * i
        line = lax.broadcasted_iota(jnp.int32, (128, 128), 0)
        found = (owner == base + line // 8) & (rank == (line // 4) % 2)
        first = jnp.sum(jnp.where(found, first_row, 0), axis=1, keepdims=True)
        across = 2 * jnp.sum(jnp.where(found, cols, 0), axis=1, keepdims=True)
        filled = across > 0
        first = jnp.where(filled, first, -10000)
        part = lax.broadcasted_iota(jnp.int32, (128, 1), 0) % 4
        token = lax.broadcasted_iota(jnp.int32, (128, TOK), 1)
        mine = first + part % 2 + (part // 2) * across
        picks[i] = (token == mine).astype(jnp.bfloat16)
        upper, lower = token - first, token - first - across
        any_part = (upper == 0) | (upper == 1) | (lower == 0) | (lower == 1)
        members[i] = any_part.astype(jnp.float32)
        return carry

    lax.fori_loop(0, SIDE, table, 0)

    share_load.wait()
    row = lax.broadcasted_iota(jnp.int32, (SHARE, SHARE), 0)
    column = lax.broadcasted_iota(jnp.int32, (SHARE, SHARE), 1)
    feature = jnp.where(column < 768, column + column // 24, (column - 768) * 25 + 24)
    unpick = (row == feature).astype(jnp.bfloat16)
    for b in range(3):
        for way, rows in ((0, (low, high)), (1, (high, low))):
            for i in range(2):
                here = final_in.at[way, b, rows[i]]
                push(here, here, final_sem.at[way, b, 1 - i], right).wait_recv()
        total = own_part[b] + final_in[0, b].astype(jnp.float32)
        total += final_in[1, b].astype(jnp.float32)
        total += token_share[:, b * 128 : (b + 1) * 128].astype(jnp.float32)
        rounded = jnp.dot(unpick, total.astype(jnp.bfloat16), preferred_element_type=jnp.float32)
        hidden[:, b * 128 : (b + 1) * 128] = rounded.astype(jnp.bfloat16)
        row_mine[0:1, b * 128 : (b + 1) * 128] = jnp.sum(rounded, axis=0, keepdims=True)
        row_mine[1:2, b * 128 : (b + 1) * 128] = jnp.sum(rounded * rounded, axis=0, keepdims=True)
    row_mine[2:] = jnp.zeros((6, TOK), jnp.float32)
    row_in[pl.ds(tp, 1)] = row_mine[...][None]
    row_copies = [
        to_row(o, row_mine, row_in, row_sem.at[0], row_sem.at[1])
        for o in (opposite, right, left_x)
    ]
    for c in row_copies:
        c.start()

    def gather_rows(i, carry):
        raws[i] = lax.dot_general(
            picks[i], hidden[...], (((1,), (1,)), ((), ())), preferred_element_type=jnp.float32
        )
        return carry

    lax.fori_loop(0, SIDE, gather_rows, 0)

    pltpu.make_async_copy(row_in.at[pl.ds(0, 3)], row_in.at[pl.ds(0, 3)], row_sem.at[0]).wait()
    row_total = row_in[0] + row_in[1] + row_in[2] + row_in[3]
    sum_row = row_total[0:1]
    square_row = row_total[1:2]
    gain = jnp.concatenate([p_gain[...], p_gain[...]], axis=0)[None]
    bias = jnp.concatenate([p_bias[...], p_bias[...]], axis=0)[None]

    def alternate(i):
        return ((i + 1) // 2) * (1 - 2 * ((i + 1) % 2))

    def fill_plane(i, carry):
        member = members[i]
        mean = jnp.sum(member * sum_row, axis=1, keepdims=True) / (4 * D)
        square = jnp.sum(member * square_row, axis=1, keepdims=True) / (4 * D)
        filled = jnp.sum(member, axis=1, keepdims=True) > 0.5
        scale = lax.rsqrt(square - mean * mean + 1e-05)
        value = ((raws[i] - mean) * scale).reshape(16, 8, SHARE) * gain + bias
        value = jnp.where(filled, value.reshape(128, SHARE), 0.0)
        slots[pl.ds(16 * i, 16)] = value[:, :768].reshape(16, 2, 4, 768).astype(jnp.bfloat16)
        end = jnp.concatenate([value[:, 768:]] * 4, axis=1)
        row = lax.broadcasted_iota(jnp.int32, (128, 128), 0)
        lane = lax.broadcasted_iota(jnp.int32, (128, 128), 1)
        end = jnp.where(row % 4 == lane // 32, end, 0.0).astype(jnp.bfloat16)
        four = lax.broadcasted_iota(jnp.int32, (32, 128), 1) // 4
        four = (four == lax.broadcasted_iota(jnp.int32, (32, 128), 0)).astype(jnp.bfloat16)
        end = jnp.dot(four, end, preferred_element_type=jnp.float32)
        slots_end[pl.ds(16 * i, 16)] = end.reshape(16, 2, 128).astype(jnp.bfloat16)
        return carry

    y = (me // 2) % SIDE
    core = me % 2

    def send(i, carry):
        to_z = lax.rem(z + alternate((15 - i % 8 - i // 8) % 8) + SIDE, SIDE)
        to_y = lax.rem(y + alternate(7 - i % 8) + SIDE, SIDE)
        for flip in range(2):
            other = shard_of(to_z, to_y, lax.rem(core + flip, 2))

            @pl.when(other != me)
            def _():
                for n, (source, into) in enumerate(((slots, out), (slots_end, out_end))):
                    pltpu.make_async_remote_copy(
                        src_ref=source.at[other],
                        dst_ref=into.at[me],
                        send_sem=send_sem.at[1 + n],
                        recv_sem=out_sem.at[n],
                        device_id={"req": other},
                        device_id_type=MESH,
                    ).start()

        return carry

    lax.fori_loop(0, SIDE, fill_plane, 0)
    lax.fori_loop(0, SIDE * SIDE, send, 0)
    for n, (source, into) in enumerate(((slots, out), (slots_end, out_end))):
        keep = pltpu.make_async_copy(source.at[me], into.at[me], own_sem.at[n])
        keep.start()
        keep.wait()
    pltpu.make_async_copy(stat_in.at[pl.ds(0, 3)], stat_in.at[pl.ds(0, 3)], stat_sem.at[1]).wait()
    pltpu.make_async_copy(row_in.at[pl.ds(0, 3)], row_in.at[pl.ds(0, 3)], row_sem.at[1]).wait()
    pltpu.make_async_copy(sums, sums, send_sem.at[0]).wait()
    for n, into in enumerate((out, out_end)):
        most = into.at[pl.ds(0, 127)]
        pltpu.make_async_copy(most, most, send_sem.at[1 + n]).wait()
        pltpu.make_async_copy(most, most, out_sem.at[n]).wait()


def finish(x, token_share, q_gain, k_gain, grids, owners, p_gain, p_bias, gathered):
    vmem = pl.BlockSpec(memory_space=pltpu.VMEM)
    bf16, f32 = jnp.bfloat16, jnp.float32
    dma = pltpu.SemaphoreType.DMA
    return pl.pallas_call(
        finish_kernel,
        out_shape=(
            jax.ShapeDtypeStruct((128, 2, 4, 768), bf16),
            jax.ShapeDtypeStruct((128, 2, 128), bf16),
        ),
        in_specs=[pl.BlockSpec(memory_space=pl.ANY)] * 2
        + [vmem] * 2
        + [pl.BlockSpec(memory_space=pltpu.SMEM)]
        + [vmem] * 3
        + [pl.BlockSpec(memory_space=pl.ANY)],
        out_specs=[pl.BlockSpec(memory_space=pl.ANY)] * 2,
        scratch_shapes=[
            pltpu.VMEM((TOK, D), bf16),
            pltpu.VMEM((SHARE, TOK), bf16),
            pltpu.VMEM((6, 128, 48, 128), bf16),
            pltpu.VMEM((128, 96, 128), bf16),
            pltpu.VMEM((128, 16, 128), bf16),
            pltpu.VMEM((128, 16, 128), f32),
            pltpu.VMEM((128, 2048), bf16),
            pltpu.VMEM((1, 128), jnp.int32),
            pltpu.VMEM((4, SHARE, 512), bf16),
            pltpu.VMEM((TOK, 1536), f32),
            pltpu.VMEM((4, 128, TOK), bf16),
            pltpu.VMEM((3, 512, 128), bf16),
            pltpu.VMEM((3, SHARE, 128), f32),
            pltpu.VMEM((2, 3, 400, 128), f32),
            pltpu.VMEM((3, 3, SHARE, 128), bf16),
            pltpu.VMEM((2, 3, 400, 128), bf16),
            pltpu.VMEM((2, 3, SHARE, 128), bf16),
            pltpu.VMEM((SHARE, TOK), bf16),
            pltpu.VMEM((8, TOK), f32),
            pltpu.VMEM((4, 8, TOK), f32),
            pltpu.VMEM((8, TOK), f32),
            pltpu.VMEM((4, 8, TOK), f32),
            pltpu.VMEM((SIDE, 128, TOK), bf16),
            pltpu.VMEM((SIDE, 128, TOK), f32),
            pltpu.VMEM((SIDE, 128, SHARE), f32),
            pltpu.VMEM((128, 2, 4, 768), bf16),
            pltpu.VMEM((128, 2, 128), bf16),
            dma((10,)),
            dma((2,)),
            dma((2,)),
            dma((2, 3)),
            dma((2, 3, 2)),
            dma((3,)),
            dma((2,)),
            dma((2,)),
        ],
        compiler_params=pltpu.CompilerParams(
            collective_id=1, has_side_effects=True, vmem_limit_bytes=60 << 20
        ),
        name="finish",
    )(x, token_share, q_gain, k_gain, grids, owners, p_gain, p_bias, gathered)


def body(tokens, norm_gain, w_qkv, q_gain, k_gain, w_out, grids, owners, proj_gain, proj_bias):
    gathered, normed, token_share = gather_weights(
        w_qkv, w_out.T, norm_gain.reshape(-1, 128), tokens
    )
    arrived, ends = finish(
        normed, token_share, q_gain.reshape(1, -1), k_gain.reshape(1, -1),
        grids.T, owners.reshape(1, -1), proj_gain, proj_bias, gathered,
    )
    return jnp.concatenate(
        [arrived.reshape(-1, 4, 768), ends.reshape(-1, 4, 32)], axis=2
    )


def solution(mesh):
    placed = (
        P("req", None),
        P(),
        P("req", "tp"),
        P("tp"),
        P("tp"),
        P("tp", "req"),
        P("req", None),
        P("req"),
        P(None, "tp"),
        P(None, "tp"),
    )
    return jax.shard_map(
        body, mesh=mesh, in_specs=placed, out_specs=P("req", None, "tp"), check_vma=False
    )
```
